32 devices in a mesh: wide: 16 (over z, y, x), narrow: 2 (over core).
Axes of the slice: x: 2, y: 2, z: 4, core: 2. Of those that a mesh axis runs over, the one named last changes fastest.
Arguments:
- data: float32 [16384, 512], P(('wide', 'narrow')), may hold values from -200 to 200, as said below
- anchors: int32 [64], replicated, may hold values from 0 to 511, as said below
Outputs:
- factor: float32 [512, 512], replicated
- coeffs: float32 [64, 512], replicated
- basis: float32 [16384, 512], P(('wide', 'narrow'))
- resid_norms: float32 [512], replicated
The draws below stay inside these ranges and needn't reach their ends.
Inputs may be any that keep to these rules, and one draw needn't show every extreme that they name: `data`: the entries are finite real numbers. `anchors`: 64 distinct column numbers.
All inputs are finite; a program needn't handle non-finite values.
Results may differ from the reference program's by a relative error of at most 0.0003.
Values sent between devices are 32-bit elements; how exact they have to be, the bound alone decides.
No kernel may reach another device: no remote copies, remote signals or barrier semaphores. Data moves between devices by JAX's collectives and lax.ppermute only.
A program may use at most 64 MiB of HBM per device.

```python
import jax
import jax.numpy as jnp
from jax import lax

N = 512
K = 64
ROWS = 16384


def column_chain(noise, rho):
    keep = (1.0 - rho * rho) ** 0.5

    def advance(previous, column):
        following = rho * previous + keep * column
        return (following, following)
    first = noise[:, 0]
    unused, rest = lax.scan(advance, first, noise[:, 1:].T)
    return jnp.concatenate([first[:, None], rest.T], axis=1)


def draw_data(key, part):
    key_a = jax.random.fold_in(key, 11)
    key_b = jax.random.fold_in(key, 12)
    noise = jnp.clip(jax.random.normal(key_a, (ROWS, N), jnp.float32), -6.0, 6.0)
    values = jnp.clip(column_chain(noise, 0.95), -6.0, 6.0)
    scales = jnp.exp(jax.random.uniform(key_b, (1, N), jnp.float32) * jnp.log(10.0))
    rising = 1.0 + 2.0 * jnp.arange(ROWS, dtype=jnp.float32)[:, None] / ROWS
    return (values * scales * rising).astype(jnp.float32)


def draw_anchors(key, part):
    order = jax.random.permutation(jax.random.fold_in(key, 21), N)
    return order[:K].astype(jnp.int32)


def setup_inputs(seed: int = 0) -> dict:
    splits = jax.random.split(jax.random.key(seed), 3)
    data = draw_data(jax.random.fold_in(splits[2], 71), 0)
    anchors = draw_anchors(jax.random.fold_in(splits[2], 71), 0)
    return dict(data=data, anchors=anchors)


def reference(data, anchors):
    high = lax.Precision.HIGHEST
    gram = lax.dot_general(data.astype(jnp.float32), data.astype(jnp.float32), (((0,), (0,)), ((), ())), precision=high, preferred_element_type=jnp.float32) / ROWS
    lower = jnp.linalg.cholesky(gram)
    factor = lower.T
    rows_k = jnp.take(gram, anchors, axis=0)
    block_k = jnp.take(rows_k, anchors, axis=1)
    chol_k = jnp.linalg.cholesky(block_k)
    coeffs = jax.scipy.linalg.cho_solve((chol_k, True), rows_k)
    basis = jax.scipy.linalg.solve_triangular(lower, data.T, lower=True).T
    data_k = jnp.take(data, anchors, axis=1)
    diff = data - jnp.dot(data_k.astype(jnp.float32), coeffs.astype(jnp.float32), precision=high, preferred_element_type=jnp.float32)
    resid_norms = jnp.sqrt(1.0 + lax.optimization_barrier(jnp.sum(diff * diff, axis=0)) / ROWS)
    return (factor, coeffs, basis, resid_norms)
```

```python
import functools

import jax
import jax.numpy as jnp
from jax import lax
from jax.experimental import pallas as pl
from jax.experimental.pallas import tpu as pltpu
from jax.sharding import PartitionSpec as P

AXES = ("wide", "narrow")
HIGH = lax.Precision.HIGHEST
NN = (((1,), (0,)), ((), ()))
NT = (((1,), (1,)), ((), ()))
TN = (((0,), (0,)), ((), ()))
T8 = 8
PANEL = 32


def mm(a, b, dims=NN):
    return lax.dot_general(a, b, dims, precision=HIGH, preferred_element_type=jnp.float32)


def rsq(p):
    r = lax.rsqrt(p)
    return r * (1.5 - (0.5 * p) * (r * r))


def lane(x, c):
    return jnp.broadcast_to(x[:, c : c + 1], (8, 128))


def sub(x, i):
    return jnp.broadcast_to(x[i : i + 1, :], (8, 128))


def splat(x, i, c):
    return jnp.broadcast_to(x[i : i + 1, c : c + 1], (8, 128))


def eliminate(sd, se, c0):
    a, e = sd[0], se[0]
    d = {(i, k): splat(a, i, c0 + k) for i in range(8) for k in range(i + 1)}
    ru = [sub(a, i) for i in range(8)]
    rw = [sub(e, i) for i in range(8)]
    cols = [[lane(x, c0 + k) for k in range(8)] for x in sd[1:]]
    nd, ne = list(sd[1:]), list(se[1:])
    row = lax.broadcasted_iota(jnp.int32, (8, 128), 0)
    u_t = jnp.zeros((8, 128), jnp.float32)
    w_t = jnp.zeros((8, 128), jnp.float32)
    for j in range(8):
        r = rsq(d[j, j])
        l = {i: d[i, j] * r for i in range(j + 1, 8)}
        for i in range(j + 1, 8):
            for k in range(j + 1, i + 1):
                d[i, k] = d[i, k] - l[i] * l[k]
        u, w = ru[j] * r, rw[j] * r
        for i in range(j + 1, 8):
            ru[i] = ru[i] - l[i] * u
            rw[i] = rw[i] - l[i] * w
        u_t = jnp.where(row == j, u, u_t)
        w_t = jnp.where(row == j, w, w_t)
        for t, c in enumerate(cols):
            low = c[j] * r
            for k in range(j + 1, 8):
                c[k] = c[k] - low * l[k]
            nd[t] = nd[t] - low * u
            ne[t] = ne[t] - low * w
    return u_t, w_t, nd, ne


def factor_block(d_ref, e_ref, size):
    tiles = PANEL // T8
    for p in range(size // PANEL):
        base = p * PANEL
        sd = [d_ref[base + 8 * t : base + 8 * t + 8, :] for t in range(tiles)]
        se = [e_ref[base + 8 * t : base + 8 * t + 8, :] for t in range(tiles)]
        us, ws = [], []
        for t in range(tiles):
            u, w, sd, se = eliminate(sd, se, base + 8 * t)
            us.append(u)
            ws.append(w)
        up = jnp.concatenate(us, axis=0)
        wp = jnp.concatenate(ws, axis=0)
        d_ref[base : base + PANEL, :] = up
        e_ref[base : base + PANEL, :] = wp
        rest = base + PANEL
        if rest < size:
            both = mm(up, jnp.concatenate([up, wp], axis=1), TN)
            d_ref[rest:size, :] = d_ref[rest:size, :] - both[rest:size, :128]
            e_ref[rest:size, :] = e_ref[rest:size, :] - both[rest:size, 128:]


def tri_upper(x):
    r = lax.broadcasted_iota(jnp.int32, x.shape, 0)
    c = lax.broadcasted_iota(jnp.int32, x.shape, 1)
    return jnp.where(r <= c, x, 0.0)


def eye(n, m):
    r = lax.broadcasted_iota(jnp.int32, (n, m), 0)
    c = lax.broadcasted_iota(jnp.int32, (n, m), 1)
    return (r == c).astype(jnp.float32)


def my_index():
    return lax.axis_index("wide") * lax.axis_size("narrow") + lax.axis_index("narrow")


def gram_kernel(x_ref, own_ref, other_ref, both_ref):
    n = 0
    for i in range(4):
        row = mm(x_ref[:, 128 * i : 128 * i + 128], x_ref[:, 128 * i :], TN)
        for j in range(4 - i):
            both_ref[n // 5, 128 * (n % 5) : 128 * (n % 5) + 128, :] = row[:, 128 * j : 128 * j + 128]
            n += 1
    bit = lax.rem(my_index(), 2)
    own_ref[...] = both_ref[bit]
    other_ref[...] = both_ref[1 - bit]


def gram_call(x):
    half = jax.ShapeDtypeStruct((640, 128), jnp.float32)
    return pl.pallas_call(
        gram_kernel,
        out_shape=(half, half),
        scratch_shapes=[pltpu.VMEM((2, 640, 128), jnp.float32)],
        compiler_params=pltpu.CompilerParams(vmem_limit_bytes=32 << 20),
        name="gram",
    )(x)


def split_kernel(own_ref, got_ref, *outs):
    q = lax.rem(my_index() // 2, 4)
    for m, out in enumerate(outs):
        rows = pl.ds(pl.multiple_of((q ^ m) * 160, 160), 160)
        out[...] = own_ref[rows, :] + got_ref[rows, :]


def split_call(own, got):
    part = jax.ShapeDtypeStruct((160, 128), jnp.float32)
    return pl.pallas_call(split_kernel, out_shape=(part,) * 4, name="split")(own, got)


def swap(x, bit, devices):
    return lax.ppermute(x, AXES, [(i, i ^ bit) for i in range(devices)])


def total_gram(x, devices):
    own, other = gram_call(x)
    parts = split_call(own, swap(other, 1, devices))
    got = [swap(parts[m], 2 * m, devices) for m in (1, 2, 3)]
    piece = (parts[0] + got[0]) + (got[1] + got[2])
    bit = 8
    while bit < devices:
        if bit * 2 < devices:
            far = [swap(piece, bit * m, devices) for m in (1, 2, 3)]
            piece = (piece + far[0]) + (far[1] + far[2])
        else:
            piece = piece + swap(piece, bit, devices)
        bit *= 4
    mine = [piece] + [swap(piece, 2 * m, devices) for m in (1, 2, 3)]
    theirs = [swap(p, 1, devices) for p in mine]
    return mine + theirs


def main_kernel(total, *refs):
    pieces, refs = refs[:8], refs[8:]
    data_ref, anc_ref, fac_ref, coef_ref, bas_ref, res_ref, d_ref, e_ref, w_ref, t_ref, g_ref = refs
    nb = 4
    me = my_index()
    core, q = lax.rem(me, 2), lax.rem(me // 2, 4)
    for m in range(8):
        at = (core ^ (m // 4)) * 640 + (q ^ (m % 4)) * 160
        g_ref[pl.ds(pl.multiple_of(at, 160), 160), :] = pieces[m][...] / total
    idx = {}
    for i in range(nb):
        for j in range(i, nb):
            idx[i, j] = len(idx)

    def blk(i, j):
        n = idx[i, j]
        return g_ref[128 * n : 128 * n + 128, :]

    lanes = lax.broadcasted_iota(jnp.int32, (64, 512), 1)
    pick = (anc_ref[...] == lanes).astype(jnp.float32)
    parts = []
    for j in range(nb):
        acc = None
        for i in range(nb):
            p = pick[:, 128 * i : 128 * i + 128]
            t = mm(p, blk(i, j)) if i <= j else mm(p, blk(j, i), NT)
            acc = t if acc is None else acc + t
        parts.append(acc)
    rows_k = jnp.concatenate(parts, axis=1)
    pad = jnp.concatenate([pick, jnp.zeros((64, 512), jnp.float32)], axis=0)
    d_ref[0:64, :] = mm(rows_k, pad, NT)
    e_ref[0:64, :] = eye(64, 128)
    factor_block(d_ref, e_ref, 64)
    linv = e_ref[0:64, 0:64]
    coeffs = mm(linv, mm(linv, rows_k), TN)
    coef_ref[...] = coeffs

    for i in range(nb):
        for j in range(i, nb):
            t_ref[128 * i : 128 * i + 128, 128 * j : 128 * j + 128] = blk(i, j)
    fac_ref[...] = jnp.zeros((512, 512), jnp.float32)
    w_ref[...] = jnp.zeros((512, 512), jnp.float32)
    for k in range(nb):
        lo, hi = 128 * k, 128 * k + 128
        d_ref[...] = t_ref[lo:hi, lo:hi]
        e_ref[...] = eye(128, 128)
        factor_block(d_ref, e_ref, 128)
        linv = e_ref[...]
        fac_ref[lo:hi, lo:hi] = tri_upper(d_ref[...])
        if k > 0:
            w_ref[lo:hi, 0:lo] = mm(linv, w_ref[lo:hi, 0:lo])
        w_ref[lo:hi, lo:hi] = linv
        if k < nb - 1:
            u = mm(linv, t_ref[lo:hi, hi:])
            fac_ref[lo:hi, hi:] = u
            for i in range(k + 1, nb):
                a = u[:, 128 * (i - k - 1) : 128 * (i - k)]
                t_ref[128 * i : 128 * i + 128, 128 * i :] = t_ref[128 * i : 128 * i + 128, 128 * i :] - mm(
                    a, u[:, 128 * (i - k - 1) :], TN
                )
                w_ref[128 * i : 128 * i + 128, 0:hi] = w_ref[128 * i : 128 * i + 128, 0:hi] - mm(
                    a, w_ref[lo:hi, 0:hi], TN
                )
        bas_ref[:, lo:hi] = mm(data_ref[:, 0:hi], w_ref[lo:hi, 0:hi], NT)
    fac = fac_ref[...]
    fac_k = mm(fac, pick, NT)
    diff = fac - mm(fac_k, coeffs)
    res_ref[...] = jnp.sqrt(1.0 + jnp.sum(diff * diff, axis=0, keepdims=True))


def main_call(pieces, data, anchors, total):
    f32 = jnp.float32
    return pl.pallas_call(
        functools.partial(main_kernel, total),
        out_shape=(
            jax.ShapeDtypeStruct((512, 512), f32),
            jax.ShapeDtypeStruct((64, 512), f32),
            jax.ShapeDtypeStruct((512, 512), f32),
            jax.ShapeDtypeStruct((1, 512), f32),
        ),
        scratch_shapes=[
            pltpu.VMEM((128, 128), f32),
            pltpu.VMEM((128, 128), f32),
            pltpu.VMEM((512, 512), f32),
            pltpu.VMEM((512, 512), f32),
            pltpu.VMEM((1280, 128), f32),
        ],
        compiler_params=pltpu.CompilerParams(vmem_limit_bytes=48 << 20),
        name="factor_fit",
    )(*pieces, data, anchors.reshape(64, 1))


def on_device(data, anchors):
    devices = lax.axis_size("wide") * lax.axis_size("narrow")
    pieces = total_gram(data, devices)
    factor, coeffs, basis, resid = main_call(pieces, data, anchors, data.shape[0] * devices)
    return (factor, coeffs, basis, resid.reshape(-1))


def solution(mesh):
    placed = (P(AXES, None), P())
    return jax.shard_map(
        on_device,
        mesh=mesh,
        in_specs=placed,
        out_specs=(P(), P(), P(AXES, None), P()),
        check_vma=False,
    )
```

```python
import functools

import jax
import jax.numpy as jnp
from jax import lax
from jax.experimental import pallas as pl
from jax.experimental.pallas import tpu as pltpu
from jax.sharding import PartitionSpec as P

AXES = ("wide", "narrow")
NN = (((1,), (0,)), ((), ()))
NT = (((1,), (1,)), ((), ()))
TN = (((0,), (0,)), ((), ()))
PANEL = 32
LEFT = (0, 0, 1, 0, 2, 1)
RIGHT = (0, 1, 0, 2, 0, 1)


def thirds(x):
    hi = x.astype(jnp.bfloat16)
    rest = x - hi.astype(jnp.float32)
    mid = rest.astype(jnp.bfloat16)
    low = (rest - mid.astype(jnp.float32)).astype(jnp.bfloat16)
    return (hi, mid, low)


def bdot(a, b, dims):
    return lax.dot_general(a, b, dims, preferred_element_type=jnp.float32)


def six(a, b, dims):
    ca, cb = dims[0][0][0], dims[0][1][0]
    left = jnp.concatenate([a[i] for i in LEFT], axis=ca)
    right = jnp.concatenate([b[i] for i in RIGHT], axis=cb)
    return bdot(left, right, dims)


def mm(a, b, dims=NN):
    return six(thirds(a), thirds(b), dims)


def mm_pick(a, pick, dims):
    return sum(bdot(t, pick, dims) for t in thirds(a))


def rsq(p):
    r = lax.rsqrt(p)
    return r * (1.5 - (0.5 * p) * (r * r))


def lane(x, c):
    return jnp.broadcast_to(x[:, c : c + 1], (8, 128))


def sub(x, i):
    return jnp.take_along_axis(x, jnp.full((8, 128), i, jnp.int32), axis=0, mode="promise_in_bounds")


def eliminate(rows, c0, s_ref):
    a = rows[0][0]
    for k in range(8):
        s_ref[8 * k : 8 * k + 8, :] = lane(a, c0 + k)
    d = {
        (i, k): jnp.broadcast_to(s_ref[8 * k + i : 8 * k + i + 1, :], (8, 128)) for i in range(8) for k in range(i + 1)
    }
    n = [lax.rsqrt(d[i, i]) for i in range(8)]
    d = {(i, k): (v * n[i]) * n[k] for (i, k), v in d.items()}
    ru = [[sub(x, i) * n[i] for x in rows[0]] for i in range(8)]
    cols = [[lane(t[0], c0 + k) * n[k] for k in range(8)] for t in rows[1:]]
    later = [list(t) for t in rows[1:]]
    row = lax.broadcasted_iota(jnp.int32, (8, 128), 0)
    out = [jnp.zeros((8, 128), jnp.float32) for _ in rows[0]]
    low = {}
    for b in (0, 4):
        below = range(b, 8)
        e = {}
        for i in below:
            e[i, 0] = d[i, b]
        p = [d[b, b]]
        for j in range(1, 4):
            for i in range(b + j, 8):
                v = p[0] * d[i, b + j] - e[i, 0] * e[b + j, 0]
                for m in range(1, j):
                    v = p[m] * v - e[i, m] * e[b + j, m]
                e[i, j] = v
            p.append(e[b + j, j])
        rho = [rsq(x) for x in p]
        root = [x * r for x, r in zip(p, rho)]
        inv = [rho[0]]
        acc = root[0]
        for j in range(1, 4):
            inv.append(rho[j] * acc)
            acc = acc * root[j]
        sig = rho[0]
        for j in range(4):
            if j:
                sig = sig * rho[j]
            for i in range(b + j + 1, 8):
                low[i, b + j] = e[i, j] * sig
        if b == 0:
            for i in range(4, 8):
                for k in range(4, i + 1):
                    x = low[i, 0] * low[k, 0] + low[i, 1] * low[k, 1]
                    y = low[i, 2] * low[k, 2] + low[i, 3] * low[k, 3]
                    d[i, k] = d[i, k] - (x + y)
        for j in range(4):
            r, at = inv[j], b + j
            u = [x * r for x in ru[at]]
            for i in range(at + 1, 8):
                ru[i] = [x - low[i, at] * y for x, y in zip(ru[i], u)]
            out = [jnp.where(row == at, y, x) for x, y in zip(out, u)]
            for t, c in enumerate(cols):
                f = c[at] * r
                for k in range(at + 1, 8):
                    c[k] = c[k] - f * low[k, at]
                later[t] = [x - f * y for x, y in zip(later[t], u)]
    return out, later


def tri_upper(x):
    r = lax.broadcasted_iota(jnp.int32, x.shape, 0)
    c = lax.broadcasted_iota(jnp.int32, x.shape, 1)
    return jnp.where(r <= c, x, 0.0)


def eye(n, m):
    r = lax.broadcasted_iota(jnp.int32, (n, m), 0)
    c = lax.broadcasted_iota(jnp.int32, (n, m), 1)
    return (r == c).astype(jnp.float32)


def cholesky_steps(t_ref, e_ref, s_ref, size, blocks, done):
    later = []
    for k in range(blocks):
        r0, c0 = k * size, k * 128
        e_ref[r0 : r0 + size, :] = eye(size, 128)
        for p in range(size // PANEL):
            base = r0 + p * PANEL
            width = blocks - k
            tiles = []
            for t in range(PANEL // 8):
                at = slice(base + 8 * t, base + 8 * t + 8)
                tiles.append(
                    [t_ref[at, c0 + 128 * w : c0 + 128 * w + 128] for w in range(width)] + [e_ref[at, :]]
                )
            outs = []
            steps = PANEL // 8
            for t in range(steps):
                out, tiles = eliminate(tiles, p * PANEL + 8 * t, s_ref.at[(p * steps + t) % 8])
                outs.append(out)
                for _ in range(-(-len(later) // (steps - t))):
                    later.pop(0)()
                yield
            full = [jnp.concatenate([o[w] for o in outs], axis=0) for w in range(width + 1)]
            for w in range(width):
                t_ref[base : base + PANEL, c0 + 128 * w : c0 + 128 * w + 128] = full[w]
            e_ref[base : base + PANEL, :] = full[width]
            split = [thirds(x) for x in full]
            left = [jnp.concatenate([s[i] for i in LEFT], axis=0) for s in split]
            right = [jnp.concatenate([s[i] for i in RIGHT], axis=0) for s in split]
            last = base + PANEL == r0 + size

            def update(w, lo, hi, flip, r0=r0, c0=c0, width=width, right=right):
                both = bdot(flip[lo:hi], jnp.concatenate(right[w:] if w == 0 else right[w:width], axis=1), NN)
                rows = slice(r0 + size * w + lo, r0 + size * w + hi)
                at = slice(c0 + 128 * w, c0 + 128 * width)
                t_ref[rows, at] = t_ref[rows, at] - both[:, : 128 * (width - w)]
                if w == 0:
                    e_ref[rows, :] = e_ref[rows, :] - both[:, 128 * width :]

            for w in range(1 if last else 0, width):
                lo = 0 if w else (p + 1) * PANEL
                flip = left[w].T
                first = w == (1 if last else 0)
                if first:
                    update(w, lo, lo + PANEL, flip)
                    lo += PANEL
                if lo < size:
                    later.append(functools.partial(update, w, lo, size, flip))
            if last:
                done(k)


def main_kernel(total, pieces, data_ref, anc_ref, fac_out, coef_out, bas_out, res_out, t_ref, e_ref, y_ref, f_ref, td_ref, ed_ref, rk_ref, cf_ref, sq_ref, s_ref, g_ref, sem):
    nb = 4
    n_rows = data_ref.shape[0]
    copies = []
    queue = []
    state = {}

    def send(src, dst, n):
        c = pltpu.make_async_copy(src, dst, sem.at[n])
        c.start()
        copies.append(c)

    place_pieces(pieces, t_ref, g_ref, total)
    lanes = lax.broadcasted_iota(jnp.int32, (64, 512), 1)
    pick = (anc_ref[...] == lanes).astype(jnp.bfloat16)

    def side_steps():
        sums = [None] * nb
        for i in range(nb):
            for j in range(i, nb):
                g = thirds(state["gram"][i, j])
                pi, pj = pick[:, 128 * i : 128 * i + 128], pick[:, 128 * j : 128 * j + 128]
                for x in g:
                    v = bdot(pi, x, NN)
                    sums[j] = v if sums[j] is None else sums[j] + v
                    if i < j:
                        v = bdot(pj, x, NT)
                        sums[i] = v if sums[i] is None else sums[i] + v
                if j % 2:
                    yield
        rows_k = jnp.concatenate(sums, axis=1)
        rk_ref[...] = rows_k
        wide = jnp.concatenate([pick, jnp.zeros((64, 512), jnp.bfloat16)], axis=0)
        td_ref[...] = mm_pick(rows_k, wide, NT)
        yield
        yield from cholesky_steps(td_ref, ed_ref, s_ref.at[1], 64, 1, lambda _: None)
        linv = thirds(ed_ref[:, 0:64])
        z = six(linv, thirds(rk_ref[...]), NN)
        yield
        cf_ref[...] = six(linv, thirds(z), TN)
        send(cf_ref, coef_out, 0)
        state["coef"] = True

    state["gram"] = {
        (i, j): t_ref[128 * i : 128 * i + 128, 128 * j : 128 * j + 128] for i in range(nb) for j in range(i, nb)
    }

    def clear(k):
        if k:
            f_ref[128 * k : 128 * k + 128, 0 : 128 * k] = jnp.zeros((128, 128 * k), jnp.float32)

    for k in range(nb):
        queue.append(functools.partial(clear, k))

    def finished(k):
        lo, hi = 128 * k, 128 * k + 128
        last = k == nb - 1
        src = data_ref if k == 0 else y_ref
        linv = thirds(e_ref[lo:hi, :])
        f_ref[lo:hi, lo:hi] = tri_upper(t_ref[lo:hi, lo:hi])
        if not last:
            f_ref[lo:hi, hi:] = t_ref[lo:hi, hi:]
            above = thirds(t_ref[lo:hi, hi:])

        def rows(n):
            at = slice(128 * n, min(128 * n + 128, n_rows))
            b = six(thirds(src[at, lo:hi]), linv, NT)
            y_ref[at, lo:hi] = b
            if not last:
                y_ref[at, hi:] = src[at, hi:] - six(thirds(b), above, NN)

        for n in range(-(-n_rows // 128)):
            queue.append(functools.partial(rows, n))
        queue.append(functools.partial(residual, k))

        def ship():
            send(f_ref.at[lo:hi, :], fac_out.at[lo:hi, :], 1 + k)
            send(y_ref.at[:, lo:hi], bas_out.at[:, lo:hi], 5 + k)

        queue.append(ship)

    def residual(k):
        lo, hi = 128 * k, 128 * k + 128
        fk = mm_pick(f_ref[lo:hi, lo:], pick[:, lo:], NT)
        diff = f_ref[lo:hi, :] - six(thirds(fk), thirds(cf_ref[...]), NN)
        v = jnp.sum(diff * diff, axis=0, keepdims=True)
        state["sq"] = v if "sq" not in state else state["sq"] + v

    main = cholesky_steps(t_ref, e_ref, s_ref.at[0], 128, nb, finished)
    side = side_steps()
    running = [main, side]
    while running:
        for s in list(running):
            try:
                next(s)
            except StopIteration:
                running.remove(s)
        if queue:
            queue.pop(0)()
    for f in queue:
        f()
    sq_ref[...] = jnp.sqrt(1.0 + state["sq"])
    send(sq_ref, res_out, 9)
    for c in copies:
        c.wait()


def place_pieces(pieces, t_ref, g_ref, total):
    me = my_index()
    core, q = lax.rem(me, 2), lax.rem(me // 2, 4)
    for m in range(8):
        at = (core ^ (m // 4)) * 640 + (q ^ (m % 4)) * 160
        g_ref[pl.ds(pl.multiple_of(at, 160), 160), :] = pieces[m][...]
    n = 0
    for i in range(4):
        for j in range(i, 4):
            x = g_ref[128 * n : 128 * n + 128, :] / total
            t_ref[128 * i : 128 * i + 128, 128 * j : 128 * j + 128] = x
            n += 1


def fit_call(pieces, data, anchors, total):
    f32 = jnp.float32
    count = len(pieces)
    rows = data.shape[0]

    def body(*refs):
        main_kernel(total, refs[:count], *refs[count:])

    vmem = pl.BlockSpec(memory_space=pltpu.VMEM)
    hbm = pl.BlockSpec(memory_space=pl.ANY)
    return pl.pallas_call(
        body,
        out_shape=(
            jax.ShapeDtypeStruct((512, 512), f32),
            jax.ShapeDtypeStruct((64, 512), f32),
            jax.ShapeDtypeStruct((rows, 512), f32),
            jax.ShapeDtypeStruct((1, 512), f32),
        ),
        in_specs=[vmem] * (count + 2),
        out_specs=(hbm,) * 4,
        scratch_shapes=[
            pltpu.VMEM((512, 512), f32),
            pltpu.VMEM((512, 128), f32),
            pltpu.VMEM((rows, 512), f32),
            pltpu.VMEM((512, 512), f32),
            pltpu.VMEM((64, 128), f32),
            pltpu.VMEM((64, 128), f32),
            pltpu.VMEM((64, 512), f32),
            pltpu.VMEM((64, 512), f32),
            pltpu.VMEM((1, 512), f32),
            pltpu.VMEM((2, 8, 64, 128), f32),
            pltpu.VMEM((1280, 128), f32),
            pltpu.SemaphoreType.DMA((10,)),
        ],
        compiler_params=pltpu.CompilerParams(vmem_limit_bytes=32 << 20),
        name="factor_fit",
    )(*pieces, data, anchors.reshape(64, 1))


def my_index():
    return lax.axis_index("wide") * lax.axis_size("narrow") + lax.axis_index("narrow")


def gram_kernel(x_hbm, own_ref, other_ref, x_ref, both_ref, sem):
    rows = x_ref.shape[0] // 4
    copies = []
    for c in range(4):
        at = pl.ds(rows * c, rows)
        copies.append(pltpu.make_async_copy(x_hbm.at[at, :], x_ref.at[at, :], sem.at[c]))
        copies[-1].start()
    for c in range(4):
        copies[c].wait()
        split = thirds(x_ref[rows * c : rows * c + rows, :])
        left = jnp.concatenate([split[i] for i in LEFT], axis=0)
        right = jnp.concatenate([split[i] for i in RIGHT], axis=0)
        n = 0
        for i in range(4):
            row = bdot(left[:, 128 * i : 128 * i + 128], right[:, 128 * i :], TN)
            for j in range(4 - i):
                at = slice(128 * (n % 5), 128 * (n % 5) + 128)
                x = row[:, 128 * j : 128 * j + 128]
                both_ref[n // 5, at, :] = x if c == 0 else both_ref[n // 5, at, :] + x
                n += 1
    bit = lax.rem(my_index(), 2)
    own_ref[...] = both_ref[bit]
    other_ref[...] = both_ref[1 - bit]


def gram_call(x):
    half = jax.ShapeDtypeStruct((640, 128), jnp.float32)
    return pl.pallas_call(
        gram_kernel,
        out_shape=(half, half, jax.ShapeDtypeStruct(x.shape, x.dtype)),
        in_specs=[pl.BlockSpec(memory_space=pltpu.HBM)],
        out_specs=(pl.BlockSpec(memory_space=pltpu.VMEM),) * 3,
        scratch_shapes=[pltpu.VMEM((2, 640, 128), jnp.float32), pltpu.SemaphoreType.DMA((4,))],
        compiler_params=pltpu.CompilerParams(vmem_limit_bytes=16 << 20),
        name="gram",
    )(x)


def split_kernel(own_ref, got_ref, *outs):
    q = lax.rem(my_index() // 2, 4)
    for m, out in enumerate(outs):
        rows = pl.ds(pl.multiple_of((q ^ m) * 160, 160), 160)
        out[...] = own_ref[rows, :] + got_ref[rows, :]


def split_call(own, got):
    part = jax.ShapeDtypeStruct((160, 128), jnp.float32)
    return pl.pallas_call(
        split_kernel,
        out_shape=(part,) * 4,
        compiler_params=pltpu.CompilerParams(vmem_limit_bytes=8 << 20),
        name="split",
    )(own, got)


def swap(x, bit, devices):
    return lax.ppermute(x, AXES, [(i, i ^ bit) for i in range(devices)])


def total_gram(x, devices):
    own, other, kept = gram_call(x)
    parts = split_call(own, swap(other, 1, devices))
    got = [swap(parts[m], 2 * m, devices) for m in (1, 2, 3)]
    piece = (parts[0] + got[0]) + (got[1] + got[2])
    bit = 8
    while bit < devices:
        if bit * 2 < devices:
            far = [swap(piece, bit * m, devices) for m in (1, 2, 3)]
            piece = (piece + far[0]) + (far[1] + far[2])
        else:
            piece = piece + swap(piece, bit, devices)
        bit *= 4
    mine = [piece] + [swap(piece, 2 * m, devices) for m in (1, 2, 3)]
    theirs = [swap(p, 1, devices) for p in mine]
    return mine + theirs, kept


def on_device(data, anchors):
    devices = lax.axis_size("wide") * lax.axis_size("narrow")
    pieces, kept = total_gram(data, devices)
    factor, coeffs, basis, resid = fit_call(pieces, kept, anchors, data.shape[0] * devices)
    return (factor, coeffs, basis, resid.reshape(-1))


def solution(mesh):
    placed = (P(AXES, None), P())
    return jax.shard_map(
        on_device,
        mesh=mesh,
        in_specs=placed,
        out_specs=(P(), P(), P(AXES, None), P()),
        check_vma=False,
    )
```

```python
import functools

import jax
import jax.numpy as jnp
from jax import lax
from jax.experimental import pallas as pl
from jax.experimental.pallas import tpu as pltpu
from jax.sharding import PartitionSpec as P

AXES = ("wide", "narrow")
NN = (((1,), (0,)), ((), ()))
NT = (((1,), (1,)), ((), ()))
TN = (((0,), (0,)), ((), ()))
PANEL = 32
HALF = 576
PIECE = HALF // 4
LEFT = (0, 0, 1, 0, 2, 1)
RIGHT = (0, 1, 0, 2, 0, 1)


def thirds(x):
    hi = x.astype(jnp.bfloat16)
    rest = x - hi.astype(jnp.float32)
    mid = rest.astype(jnp.bfloat16)
    low = (rest - mid.astype(jnp.float32)).astype(jnp.bfloat16)
    return (hi, mid, low)


def bdot(a, b, dims):
    return lax.dot_general(a, b, dims, preferred_element_type=jnp.float32)


def six(a, b, dims):
    ca, cb = dims[0][0][0], dims[0][1][0]
    left = jnp.concatenate([a[i] for i in LEFT], axis=ca)
    right = jnp.concatenate([b[i] for i in RIGHT], axis=cb)
    return bdot(left, right, dims)


def mm(a, b, dims=NN):
    return six(thirds(a), thirds(b), dims)


def mm_pick(a, pick, dims):
    return sum(bdot(t, pick, dims) for t in thirds(a))


def rsq(p):
    r = lax.rsqrt(p)
    return r * (1.5 - (0.5 * p) * (r * r))


def lane(x, c):
    return jnp.broadcast_to(x[:, c : c + 1], (8, 128))


def sub(x, i):
    return jnp.take_along_axis(x, jnp.full((8, 128), i, jnp.int32), axis=0, mode="promise_in_bounds")


def eliminate(rows, c0, s_ref):
    a = rows[0][0]
    for k in range(8):
        s_ref[8 * k : 8 * k + 8, :] = lane(a, c0 + k)
    d = {
        (i, k): jnp.broadcast_to(s_ref[8 * k + i : 8 * k + i + 1, :], (8, 128)) for i in range(8) for k in range(i + 1)
    }
    n = [lax.rsqrt(d[i, i]) for i in range(8)]
    d = {(i, k): (v * n[i]) * n[k] for (i, k), v in d.items()}
    ru = [[sub(x, i) * n[i] for x in rows[0]] for i in range(8)]
    cols = [[lane(t[0], c0 + k) * n[k] for k in range(8)] for t in rows[1:]]
    later = [list(t) for t in rows[1:]]
    row = lax.broadcasted_iota(jnp.int32, (8, 128), 0)
    out = [jnp.zeros((8, 128), jnp.float32) for _ in rows[0]]
    low = {}
    for b in (0, 4):
        below = range(b, 8)
        e = {}
        for i in below:
            e[i, 0] = d[i, b]
        p = [d[b, b]]
        for j in range(1, 4):
            for i in range(b + j, 8):
                v = p[0] * d[i, b + j] - e[i, 0] * e[b + j, 0]
                for m in range(1, j):
                    v = p[m] * v - e[i, m] * e[b + j, m]
                e[i, j] = v
            p.append(e[b + j, j])
        rho = [rsq(x) for x in p]
        root = [x * r for x, r in zip(p, rho)]
        inv = [rho[0]]
        acc = root[0]
        for j in range(1, 4):
            inv.append(rho[j] * acc)
            acc = acc * root[j]
        sig = rho[0]
        for j in range(4):
            if j:
                sig = sig * rho[j]
            for i in range(b + j + 1, 8):
                low[i, b + j] = e[i, j] * sig
        if b == 0:
            for i in range(4, 8):
                for k in range(4, i + 1):
                    x = low[i, 0] * low[k, 0] + low[i, 1] * low[k, 1]
                    y = low[i, 2] * low[k, 2] + low[i, 3] * low[k, 3]
                    d[i, k] = d[i, k] - (x + y)
        for j in range(4):
            r, at = inv[j], b + j
            u = [x * r for x in ru[at]]
            for i in range(at + 1, 8):
                ru[i] = [x - low[i, at] * y for x, y in zip(ru[i], u)]
            out = [jnp.where(row == at, y, x) for x, y in zip(out, u)]
            for t, c in enumerate(cols):
                f = c[at] * r
                for k in range(at + 1, 8):
                    c[k] = c[k] - f * low[k, at]
                later[t] = [x - f * y for x, y in zip(later[t], u)]
    return out, later


def tri_upper(x):
    r = lax.broadcasted_iota(jnp.int32, x.shape, 0)
    c = lax.broadcasted_iota(jnp.int32, x.shape, 1)
    return jnp.where(r <= c, x, 0.0)


def eye(n, m):
    r = lax.broadcasted_iota(jnp.int32, (n, m), 0)
    c = lax.broadcasted_iota(jnp.int32, (n, m), 1)
    return (r == c).astype(jnp.float32)


def cholesky_steps(t_ref, e_ref, s_ref, size, blocks, done):
    later = []
    steps = PANEL // 8

    def apply(inverse, rows, c0, width, both):
        at = slice(c0 + 128, c0 + 128 * width)
        parts = ([t_ref[rows, at]] if width > 1 else []) + ([e_ref[rows, :]] if both else [])
        if not parts:
            return
        x = lax.dot_general(
            inverse,
            jnp.concatenate(parts, axis=1),
            NN,
            precision=lax.Precision.HIGHEST,
            preferred_element_type=jnp.float32,
        )
        if width > 1:
            t_ref[rows, at] = x[:, : 128 * (width - 1)]
        if both:
            e_ref[rows, :] = x[:, 128 * (width - 1) :]

    def sides(x):
        split = thirds(x)
        left = jnp.concatenate([split[i] for i in LEFT], axis=0).T
        return left, jnp.concatenate([split[i] for i in RIGHT], axis=0)

    def update(ref, rows, at, left, right):
        ref[rows, at] = ref[rows, at] - bdot(left, right, NN)

    for k in range(blocks):
        r0, c0, width = k * size, k * 128, blocks - k
        e_ref[r0 : r0 + size, :] = eye(size, 128)
        here = slice(c0, c0 + 128)
        for p in range(size // PANEL):
            base = r0 + p * PANEL
            rows = slice(base, base + PANEL)
            tiles = []
            unit = eye(PANEL, 128)
            for t in range(steps):
                tiles.append([t_ref[base + 8 * t : base + 8 * t + 8, here], unit[8 * t : 8 * t + 8, :]])
            outs = []
            for t in range(steps):
                out, tiles = eliminate(tiles, p * PANEL + 8 * t, s_ref.at[(p * steps + t) % 8])
                outs.append(out)
                for _ in range(-(-len(later) // (steps - t))):
                    later.pop(0)()
                yield
            up = jnp.concatenate([o[0] for o in outs], axis=0)
            inverse = jnp.concatenate([o[1] for o in outs], axis=0)[:, :PANEL]
            t_ref[rows, here] = up
            nxt = (p + 1) * PANEL
            last = nxt == size
            if not last:
                left, right = sides(up)
                update(t_ref, slice(base + PANEL, base + 2 * PANEL), here, left[nxt : nxt + PANEL], right)
                if nxt + PANEL < size:
                    later.append(
                        functools.partial(
                            update, t_ref, slice(base + 2 * PANEL, r0 + size), here, left[nxt + PANEL : size], right
                        )
                    )

            def others(left=None, rows=rows, r0=r0, c0=c0, width=width, nxt=nxt, inverse=inverse):
                cols = slice(c0 + 128, c0 + 128 * width)
                w_left, w_right = [], []
                for w in range(1, width):
                    a, b = sides(t_ref[rows, c0 + 128 * w : c0 + 128 * w + 128])
                    w_left.append(a)
                    w_right.append(b)
                if left is not None:
                    e_left, e_right = sides(e_ref[rows, :])
                    in_block = slice(r0 + nxt, r0 + size)
                    if width > 1:
                        update(t_ref, in_block, cols, left[nxt:size], jnp.concatenate(w_right, axis=1))
                    update(e_ref, in_block, slice(0, 128), left[nxt:size], e_right)
                return w_left, w_right

            def below(w_left, w_right, r0=r0, c0=c0, width=width, skip=False):
                for w in range(1, width):
                    at = slice(c0 + 128 * w, c0 + 128 * width)
                    lo = 0
                    right = jnp.concatenate(w_right[w - 1 :], axis=1)
                    if w == 1 and skip:
                        first = slice(r0 + size, r0 + size + PANEL)
                        if width > 2:
                            update(t_ref, first, slice(at.start + 128, at.stop), w_left[0][:PANEL], right[:, 128:])
                        lo = PANEL
                    update(t_ref, slice(r0 + size * w + lo, r0 + size * w + size), at, w_left[w - 1][lo:size], right)

            if last:
                apply(inverse, rows, c0, width, True)
                if width > 1:
                    w_left, w_right = others()
                    update(
                        t_ref,
                        slice(r0 + size, r0 + size + PANEL),
                        slice(c0 + 128, c0 + 256),
                        w_left[0][:PANEL],
                        w_right[0],
                    )
                    later.append(functools.partial(below, w_left, w_right, skip=True))
                done(k)
            else:

                def second(
                    left=left, others=others, below=below, inverse=inverse, rows=rows, c0=c0, width=width
                ):
                    apply(inverse, rows, c0, width, True)
                    held.append(others(left))

                def third(below=below):
                    below(*held.pop(0))

                held = []
                later.append(second)
                if width > 1:
                    later.append(third)


def main_kernel(total, pieces, data_ref, anc_ref, fac_out, coef_out, bas_out, res_out, t_ref, e_ref, y_ref, f_ref, td_ref, ed_ref, rk_ref, cf_ref, sq_ref, s_ref, g_ref, sem):
    nb = 4
    n_rows = data_ref.shape[0]
    copies = []
    queue = []
    state = {}

    def send(src, dst, n):
        c = pltpu.make_async_copy(src, dst, sem.at[n])
        c.start()
        copies.append(c)

    place_pieces(pieces, t_ref, g_ref, total)
    lanes = lax.broadcasted_iota(jnp.int32, (64, 512), 1)
    pick = (anc_ref[...] == lanes).astype(jnp.bfloat16)

    def side_steps():
        sums = [None] * nb
        for i in range(nb):
            for j in range(i, nb):
                whole = state["gram"][i, j]
                if i == j:
                    r = lax.broadcasted_iota(jnp.int32, (128, 128), 0)
                    c = lax.broadcasted_iota(jnp.int32, (128, 128), 1)
                    whole = jnp.where((r >= 64) & (c < 64), whole.T, whole)
                g = thirds(whole)
                pi, pj = pick[:, 128 * i : 128 * i + 128], pick[:, 128 * j : 128 * j + 128]
                for x in g:
                    v = bdot(pi, x, NN)
                    sums[j] = v if sums[j] is None else sums[j] + v
                    if i < j:
                        v = bdot(pj, x, NT)
                        sums[i] = v if sums[i] is None else sums[i] + v
                if j % 2:
                    yield
        rows_k = jnp.concatenate(sums, axis=1)
        rk_ref[...] = rows_k
        wide = jnp.concatenate([pick, jnp.zeros((64, 512), jnp.bfloat16)], axis=0)
        td_ref[...] = mm_pick(rows_k, wide, NT)
        yield
        yield from cholesky_steps(td_ref, ed_ref, s_ref.at[1], 64, 1, lambda _: None)
        linv = thirds(ed_ref[:, 0:64])
        z = six(linv, thirds(rk_ref[...]), NN)
        yield
        cf_ref[...] = six(linv, thirds(z), TN)
        send(cf_ref, coef_out, 0)
        state["coef"] = True

    state["gram"] = {
        (i, j): t_ref[128 * i : 128 * i + 128, 128 * j : 128 * j + 128] for i in range(nb) for j in range(i, nb)
    }

    def clear(k):
        if k:
            f_ref[128 * k : 128 * k + 128, 0 : 128 * k] = jnp.zeros((128, 128 * k), jnp.float32)

    for k in range(nb):
        queue.append(functools.partial(clear, k))

    def finished(k):
        lo, hi = 128 * k, 128 * k + 128
        last = k == nb - 1
        src = data_ref if k == 0 else y_ref
        linv = thirds(e_ref[lo:hi, :])
        f_ref[lo:hi, lo:hi] = tri_upper(t_ref[lo:hi, lo:hi])
        if not last:
            f_ref[lo:hi, hi:] = t_ref[lo:hi, hi:]
            above = thirds(t_ref[lo:hi, hi:])

        def rows(n):
            at = slice(128 * n, min(128 * n + 128, n_rows))
            b = six(thirds(src[at, lo:hi]), linv, NT)
            y_ref[at, lo:hi] = b
            if not last:
                y_ref[at, hi:] = src[at, hi:] - six(thirds(b), above, NN)

        for n in range(-(-n_rows // 128)):
            queue.append(functools.partial(rows, n))
        queue.append(functools.partial(residual, k))

        def ship():
            send(f_ref.at[lo:hi, :], fac_out.at[lo:hi, :], 1 + k)
            send(y_ref.at[:, lo:hi], bas_out.at[:, lo:hi], 5 + k)

        queue.append(ship)

    def residual(k):
        lo, hi = 128 * k, 128 * k + 128
        fk = mm_pick(f_ref[lo:hi, lo:], pick[:, lo:], NT)
        diff = f_ref[lo:hi, :] - six(thirds(fk), thirds(cf_ref[...]), NN)
        v = jnp.sum(diff * diff, axis=0, keepdims=True)
        state["sq"] = v if "sq" not in state else state["sq"] + v

    main = cholesky_steps(t_ref, e_ref, s_ref.at[0], 128, nb, finished)
    side = side_steps()
    running = [main, side]
    while running:
        for s in list(running):
            try:
                next(s)
            except StopIteration:
                running.remove(s)
        if queue:
            queue.pop(0)()
    for f in queue:
        f()
    sq_ref[...] = jnp.sqrt(1.0 + state["sq"])
    send(sq_ref, res_out, 9)
    for c in copies:
        c.wait()


def place_pieces(pieces, t_ref, g_ref, total):
    me = my_index()
    core, q = lax.rem(me, 2), lax.rem(me // 2, 4)
    for m in range(8):
        at = (core ^ (m // 4)) * HALF + (q ^ (m % 4)) * PIECE
        g_ref[pl.ds(pl.multiple_of(at, PIECE), PIECE), :] = pieces[m][...] / total
    n = 0
    for i in range(4):
        rows = slice(128 * i, 128 * i + 64)
        t_ref[rows, 128 * i : 128 * i + 128] = g_ref[64 * n : 64 * n + 64, :]
        n += 1
        for j in range(i + 1, 4):
            t_ref[128 * i : 128 * i + 128, 128 * j : 128 * j + 128] = g_ref[64 * n : 64 * n + 128, :]
            n += 2
    for i in range(4):
        x = g_ref[64 * (n + i // 2) : 64 * (n + i // 2) + 64, :]
        if i % 2 == 0:
            x = pltpu.roll(x, 64, 1)
        t_ref[128 * i + 64 : 128 * i + 128, 128 * i : 128 * i + 128] = x


def fit_call(pieces, data, anchors, total):
    f32 = jnp.float32
    count = len(pieces)
    rows = data.shape[0]

    def body(*refs):
        main_kernel(total, refs[:count], *refs[count:])

    vmem = pl.BlockSpec(memory_space=pltpu.VMEM)
    hbm = pl.BlockSpec(memory_space=pl.ANY)
    return pl.pallas_call(
        body,
        out_shape=(
            jax.ShapeDtypeStruct((512, 512), f32),
            jax.ShapeDtypeStruct((64, 512), f32),
            jax.ShapeDtypeStruct((rows, 512), f32),
            jax.ShapeDtypeStruct((1, 512), f32),
        ),
        in_specs=[vmem] * (count + 2),
        out_specs=(hbm,) * 4,
        scratch_shapes=[
            pltpu.VMEM((512, 512), f32),
            pltpu.VMEM((512, 128), f32),
            pltpu.VMEM((rows, 512), f32),
            pltpu.VMEM((512, 512), f32),
            pltpu.VMEM((64, 128), f32),
            pltpu.VMEM((64, 128), f32),
            pltpu.VMEM((64, 512), f32),
            pltpu.VMEM((64, 512), f32),
            pltpu.VMEM((1, 512), f32),
            pltpu.VMEM((2, 8, 64, 128), f32),
            pltpu.VMEM((2 * HALF, 128), f32),
            pltpu.SemaphoreType.DMA((10,)),
        ],
        compiler_params=pltpu.CompilerParams(vmem_limit_bytes=32 << 20),
        name="factor_fit",
    )(*pieces, data, anchors.reshape(64, 1))


def my_index():
    return lax.axis_index("wide") * lax.axis_size("narrow") + lax.axis_index("narrow")


def gram_kernel(x_hbm, own_ref, other_ref, x_ref, both_ref, sem):
    rows = x_ref.shape[0] // 4
    copies = []
    for c in range(4):
        at = pl.ds(rows * c, rows)
        copies.append(pltpu.make_async_copy(x_hbm.at[at, :], x_ref.at[at, :], sem.at[c]))
        copies[-1].start()
    for c in copies:
        c.wait()
    x = x_ref[...]

    def put(n, unit):
        both_ref[n // 9, 64 * (n % 9) : 64 * (n % 9) + 64, :] = unit

    n = 0
    corners = []
    for i in range(4):
        row = mm(x[:, 128 * i : 128 * i + 128], x[:, 128 * i :], TN)
        for j in range(4 - i):
            put(n, row[:64, 128 * j : 128 * j + 128])
            n += 1
            if j:
                put(n, row[64:, 128 * j : 128 * j + 128])
                n += 1
        corners.append(row[64:, :128])
    lanes = lax.broadcasted_iota(jnp.int32, (64, 128), 1)
    for i in (0, 2):
        put(n, jnp.where(lanes < 64, pltpu.roll(corners[i], 64, 1), corners[i + 1]))
        n += 1
    bit = lax.rem(my_index(), 2)
    own_ref[...] = both_ref[bit]
    other_ref[...] = both_ref[1 - bit]


def gram_call(x):
    half = jax.ShapeDtypeStruct((HALF, 128), jnp.float32)
    return pl.pallas_call(
        gram_kernel,
        out_shape=(half, half, jax.ShapeDtypeStruct(x.shape, x.dtype)),
        in_specs=[pl.BlockSpec(memory_space=pltpu.HBM)],
        out_specs=(pl.BlockSpec(memory_space=pltpu.VMEM),) * 3,
        scratch_shapes=[pltpu.VMEM((2, HALF, 128), jnp.float32), pltpu.SemaphoreType.DMA((4,))],
        compiler_params=pltpu.CompilerParams(vmem_limit_bytes=16 << 20),
        name="gram",
    )(pltpu.with_memory_space_constraint(x, pltpu.HBM))


def split_kernel(own_ref, got_ref, *outs):
    q = lax.rem(my_index() // 2, 4)
    for m, out in enumerate(outs):
        rows = pl.ds(pl.multiple_of((q ^ m) * PIECE, PIECE), PIECE)
        out[...] = own_ref[rows, :] + got_ref[rows, :]


def split_call(own, got):
    part = jax.ShapeDtypeStruct((PIECE, 128), jnp.float32)
    return pl.pallas_call(
        split_kernel,
        out_shape=(part,) * 4,
        compiler_params=pltpu.CompilerParams(vmem_limit_bytes=8 << 20),
        name="split",
    )(own, got)


def swap(x, bit, devices):
    return lax.ppermute(x, AXES, [(i, i ^ bit) for i in range(devices)])


def total_gram(x, devices):
    own, other, kept = gram_call(x)
    parts = split_call(own, swap(other, 1, devices))
    got = [swap(parts[m], 2 * m, devices) for m in (1, 2, 3)]
    piece = (parts[0] + got[0]) + (got[1] + got[2])
    bit = 8
    while bit < devices:
        if bit * 2 < devices:
            far = [swap(piece, bit * m, devices) for m in (1, 2, 3)]
            piece = (piece + far[0]) + (far[1] + far[2])
        else:
            piece = piece + swap(piece, bit, devices)
        bit *= 4
    mine = [piece] + [swap(piece, 2 * m, devices) for m in (1, 2, 3)]
    theirs = [swap(p, 1, devices) for p in mine]
    return mine + theirs, kept


def on_device(data, anchors):
    devices = lax.axis_size("wide") * lax.axis_size("narrow")
    pieces, kept = total_gram(data, devices)
    factor, coeffs, basis, resid = fit_call(pieces, kept, anchors, data.shape[0] * devices)
    return (factor, coeffs, basis, resid.reshape(-1))


def solution(mesh):
    placed = (P(AXES, None), P())
    return jax.shard_map(
        on_device,
        mesh=mesh,
        in_specs=placed,
        out_specs=(P(), P(), P(AXES, None), P()),
        check_vma=False,
    )
```

```python
import functools

import jax
import jax.numpy as jnp
from jax import lax
from jax.experimental import pallas as pl
from jax.experimental.pallas import tpu as pltpu
from jax.sharding import PartitionSpec as P

AXES = ("wide", "narrow")
NN = (((1,), (0,)), ((), ()))
NT = (((1,), (1,)), ((), ()))
TN = (((0,), (0,)), ((), ()))
PANEL = 32
HALF = 576
PIECE = HALF // 4
LEFT = (0, 0, 1, 0, 2, 1)
RIGHT = (0, 1, 0, 2, 0, 1)


def thirds(x):
    hi = x.astype(jnp.bfloat16)
    rest = x - hi.astype(jnp.float32)
    mid = rest.astype(jnp.bfloat16)
    low = (rest - mid.astype(jnp.float32)).astype(jnp.bfloat16)
    return (hi, mid, low)


def bdot(a, b, dims):
    return lax.dot_general(a, b, dims, preferred_element_type=jnp.float32)


def six(a, b, dims):
    ca, cb = dims[0][0][0], dims[0][1][0]
    left = jnp.concatenate([a[i] for i in LEFT], axis=ca)
    right = jnp.concatenate([b[i] for i in RIGHT], axis=cb)
    return bdot(left, right, dims)


def mm(a, b, dims=NN):
    return six(thirds(a), thirds(b), dims)


def mm_pick(a, pick, dims):
    return sum(bdot(t, pick, dims) for t in thirds(a))


def rsq(p):
    r = lax.rsqrt(p)
    return r


def lane(x, c):
    return jnp.broadcast_to(x[:, c : c + 1], (8, 128))


def sub(x, i):
    return jnp.take_along_axis(x, jnp.full((8, 128), i, jnp.int32), axis=0, mode="promise_in_bounds")


def eliminate(rows, c0, s_ref):
    a = rows[0][0]
    for k in range(8):
        s_ref[8 * k : 8 * k + 8, :] = lane(a, c0 + k)
    d = {
        (i, k): jnp.broadcast_to(s_ref[8 * k + i : 8 * k + i + 1, :], (8, 128)) for i in range(8) for k in range(i + 1)
    }
    n = [lax.rsqrt(d[i, i]) for i in range(8)]
    d = {(i, k): (v * n[i]) * n[k] for (i, k), v in d.items()}
    ru = [[sub(x, i) * n[i] for x in rows[0]] for i in range(8)]
    cols = [[lane(t[0], c0 + k) * n[k] for k in range(8)] for t in rows[1:]]
    later = [list(t) for t in rows[1:]]
    row = lax.broadcasted_iota(jnp.int32, (8, 128), 0)
    out = [jnp.zeros((8, 128), jnp.float32) for _ in rows[0]]
    low = {}
    for b in (0, 4):
        below = range(b, 8)
        e = {}
        for i in below:
            e[i, 0] = d[i, b]
        p = [d[b, b]]
        for j in range(1, 4):
            for i in range(b + j, 8):
                v = p[0] * d[i, b + j] - e[i, 0] * e[b + j, 0]
                for m in range(1, j):
                    v = p[m] * v - e[i, m] * e[b + j, m]
                e[i, j] = v
            p.append(e[b + j, j])
        rho = [rsq(x) for x in p]
        root = [x * r for x, r in zip(p, rho)]
        inv = [rho[0]]
        acc = root[0]
        for j in range(1, 4):
            inv.append(rho[j] * acc)
            acc = acc * root[j]
        sig = rho[0]
        for j in range(4):
            if j:
                sig = sig * rho[j]
            for i in range(b + j + 1, 8):
                low[i, b + j] = e[i, j] * sig
        if b == 0:
            for i in range(4, 8):
                for k in range(4, i + 1):
                    x = low[i, 0] * low[k, 0] + low[i, 1] * low[k, 1]
                    y = low[i, 2] * low[k, 2] + low[i, 3] * low[k, 3]
                    d[i, k] = d[i, k] - (x + y)
        for j in range(4):
            r, at = inv[j], b + j
            u = [x * r for x in ru[at]]
            for i in range(at + 1, 8):
                ru[i] = [x - low[i, at] * y for x, y in zip(ru[i], u)]
            out = [jnp.where(row == at, y, x) for x, y in zip(out, u)]
            for t, c in enumerate(cols):
                f = c[at] * r
                for k in range(at + 1, 8):
                    c[k] = c[k] - f * low[k, at]
                later[t] = [x - f * y for x, y in zip(later[t], u)]
    return out, later


def tri_upper(x):
    r = lax.broadcasted_iota(jnp.int32, x.shape, 0)
    c = lax.broadcasted_iota(jnp.int32, x.shape, 1)
    return jnp.where(r <= c, x, 0.0)


def eye(n, m):
    r = lax.broadcasted_iota(jnp.int32, (n, m), 0)
    c = lax.broadcasted_iota(jnp.int32, (n, m), 1)
    return (r == c).astype(jnp.float32)


def cholesky_steps(t_ref, e_ref, s_ref, size, blocks, done):
    later = []
    steps = PANEL // 8

    def apply(inverse, rows, c0, width, both):
        at = slice(c0 + 128, c0 + 128 * width)
        parts = ([t_ref[rows, at]] if width > 1 else []) + ([e_ref[rows, :]] if both else [])
        if not parts:
            return
        x = lax.dot_general(
            inverse,
            jnp.concatenate(parts, axis=1),
            NN,
            precision=lax.Precision.HIGHEST,
            preferred_element_type=jnp.float32,
        )
        if width > 1:
            t_ref[rows, at] = x[:, : 128 * (width - 1)]
        if both:
            e_ref[rows, :] = x[:, 128 * (width - 1) :]

    def sides(x):
        split = thirds(x)
        left = jnp.concatenate([split[i] for i in LEFT], axis=0).T
        return left, jnp.concatenate([split[i] for i in RIGHT], axis=0)

    def update(ref, rows, at, left, right):
        ref[rows, at] = ref[rows, at] - bdot(left, right, NN)

    for k in range(blocks):
        r0, c0, width = k * size, k * 128, blocks - k
        e_ref[r0 : r0 + size, :] = eye(size, 128)
        here = slice(c0, c0 + 128)
        for p in range(size // PANEL):
            base = r0 + p * PANEL
            rows = slice(base, base + PANEL)
            tiles = []
            unit = eye(PANEL, 128)
            for t in range(steps):
                tiles.append([t_ref[base + 8 * t : base + 8 * t + 8, here], unit[8 * t : 8 * t + 8, :]])
            outs = []
            for t in range(steps):
                out, tiles = eliminate(tiles, p * PANEL + 8 * t, s_ref.at[(p * steps + t) % 8])
                outs.append(out)
                for _ in range(-(-len(later) // (steps - t))):
                    later.pop(0)()
                yield
            up = jnp.concatenate([o[0] for o in outs], axis=0)
            inverse = jnp.concatenate([o[1] for o in outs], axis=0)[:, :PANEL]
            t_ref[rows, here] = up
            nxt = (p + 1) * PANEL
            last = nxt == size
            if not last:
                left, right = sides(up)
                update(t_ref, slice(base + PANEL, base + 2 * PANEL), here, left[nxt : nxt + PANEL], right)
                if nxt + PANEL < size:
                    later.append(
                        functools.partial(
                            update, t_ref, slice(base + 2 * PANEL, r0 + size), here, left[nxt + PANEL : size], right
                        )
                    )

            def others(left=None, rows=rows, r0=r0, c0=c0, width=width, nxt=nxt, inverse=inverse):
                cols = slice(c0 + 128, c0 + 128 * width)
                w_left, w_right = [], []
                for w in range(1, width):
                    a, b = sides(t_ref[rows, c0 + 128 * w : c0 + 128 * w + 128])
                    w_left.append(a)
                    w_right.append(b)
                if left is not None:
                    e_left, e_right = sides(e_ref[rows, :])
                    in_block = slice(r0 + nxt, r0 + size)
                    if width > 1:
                        update(t_ref, in_block, cols, left[nxt:size], jnp.concatenate(w_right, axis=1))
                    update(e_ref, in_block, slice(0, 128), left[nxt:size], e_right)
                return w_left, w_right

            def below(w_left, w_right, r0=r0, c0=c0, width=width, skip=False):
                for w in range(1, width):
                    at = slice(c0 + 128 * w, c0 + 128 * width)
                    lo = 0
                    right = jnp.concatenate(w_right[w - 1 :], axis=1)
                    if w == 1 and skip:
                        first = slice(r0 + size, r0 + size + PANEL)
                        if width > 2:
                            update(t_ref, first, slice(at.start + 128, at.stop), w_left[0][:PANEL], right[:, 128:])
                        lo = PANEL
                    update(t_ref, slice(r0 + size * w + lo, r0 + size * w + size), at, w_left[w - 1][lo:size], right)

            if last:
                apply(inverse, rows, c0, width, True)
                if width > 1:
                    w_left, w_right = others()
                    update(
                        t_ref,
                        slice(r0 + size, r0 + size + PANEL),
                        slice(c0 + 128, c0 + 256),
                        w_left[0][:PANEL],
                        w_right[0],
                    )
                    later.append(functools.partial(below, w_left, w_right, skip=True))
                done(k)
            else:

                def second(
                    left=left, others=others, below=below, inverse=inverse, rows=rows, c0=c0, width=width
                ):
                    apply(inverse, rows, c0, width, True)
                    held.append(others(left))

                def third(below=below):
                    below(*held.pop(0))

                held = []
                later.append(second)
                if width > 1:
                    later.append(third)


def main_kernel(total, pieces, data_ref, anc_ref, fac_out, coef_out, bas_out, res_out, t_ref, e_ref, y_ref, f_ref, td_ref, ed_ref, rk_ref, cf_ref, sq_ref, s_ref, g_ref, sem):
    nb = 4
    n_rows = data_ref.shape[0]
    copies = []
    queue = []
    state = {}

    def send(src, dst):
        c = pltpu.make_async_copy(src, dst, sem.at[len(copies)])
        c.start()
        copies.append(c)

    place_pieces(pieces, t_ref, g_ref, total)
    lanes = lax.broadcasted_iota(jnp.int32, (64, 512), 1)
    pick = (anc_ref[...] == lanes).astype(jnp.bfloat16)

    def side_steps():
        sums = [None] * nb
        for i in range(nb):
            for j in range(i, nb):
                whole = state["gram"][i, j]
                if i == j:
                    r = lax.broadcasted_iota(jnp.int32, (128, 128), 0)
                    c = lax.broadcasted_iota(jnp.int32, (128, 128), 1)
                    whole = jnp.where((r >= 64) & (c < 64), whole.T, whole)
                g = thirds(whole)
                pi, pj = pick[:, 128 * i : 128 * i + 128], pick[:, 128 * j : 128 * j + 128]
                for x in g:
                    v = bdot(pi, x, NN)
                    sums[j] = v if sums[j] is None else sums[j] + v
                    if i < j:
                        v = bdot(pj, x, NT)
                        sums[i] = v if sums[i] is None else sums[i] + v
                if j % 2:
                    yield
        rows_k = jnp.concatenate(sums, axis=1)
        rk_ref[...] = rows_k
        wide = jnp.concatenate([pick, jnp.zeros((64, 512), jnp.bfloat16)], axis=0)
        td_ref[...] = mm_pick(rows_k, wide, NT)
        yield
        yield from cholesky_steps(td_ref, ed_ref, s_ref.at[1], 64, 1, lambda _: None)
        linv = thirds(ed_ref[:, 0:64])
        z = six(linv, thirds(rk_ref[...]), NN)
        yield
        cf_ref[...] = six(linv, thirds(z), TN)
        send(cf_ref, coef_out)
        state["coef"] = True

    state["gram"] = {
        (i, j): t_ref[128 * i : 128 * i + 128, 128 * j : 128 * j + 128] for i in range(nb) for j in range(i, nb)
    }

    def clear(k):
        if k:
            f_ref[128 * k : 128 * k + 128, 0 : 128 * k] = jnp.zeros((128, 128 * k), jnp.float32)

    for k in range(nb):
        queue.append(functools.partial(clear, k))

    def finished(k):
        lo, hi = 128 * k, 128 * k + 128
        last = k == nb - 1
        src = data_ref if k == 0 else y_ref
        linv = thirds(e_ref[lo:hi, :])
        f_ref[lo:hi, lo:hi] = tri_upper(t_ref[lo:hi, lo:hi])
        if not last:
            f_ref[lo:hi, hi:] = t_ref[lo:hi, hi:]
            above = thirds(t_ref[lo:hi, hi:])

        def rows(n):
            at = slice(128 * n, min(128 * n + 128, n_rows))
            b = six(thirds(src[at, lo:hi]), linv, NT)
            y_ref[at, lo:hi] = b
            if not last:
                y_ref[at, hi:] = src[at, hi:] - six(thirds(b), above, NN)

        def ship_factor():
            send(f_ref.at[lo:hi, :], fac_out.at[lo:hi, :])

        def ship_basis(n):
            at = slice(128 * n, min(128 * n + 128, n_rows))
            send(y_ref.at[at, lo:hi], bas_out.at[at, lo:hi])

        queue.append(ship_factor)
        if last:
            queue.append(functools.partial(residual, k))
        for n in range(-(-n_rows // 128)):
            queue.append(functools.partial(rows, n))
            queue.append(functools.partial(ship_basis, n))
        if not last:
            queue.append(functools.partial(residual, k))

    def residual(k):
        lo, hi = 128 * k, 128 * k + 128
        fk = mm_pick(f_ref[lo:hi, lo:], pick[:, lo:], NT)
        diff = f_ref[lo:hi, :] - six(thirds(fk), thirds(cf_ref[...]), NN)
        v = jnp.sum(diff * diff, axis=0, keepdims=True)
        state["sq"] = v if "sq" not in state else state["sq"] + v

    main = cholesky_steps(t_ref, e_ref, s_ref.at[0], 128, nb, finished)
    side = side_steps()
    running = [main, side]
    while running:
        for s in list(running):
            try:
                next(s)
            except StopIteration:
                running.remove(s)
        if queue:
            queue.pop(0)()
    for f in queue:
        f()
    sq_ref[...] = jnp.sqrt(1.0 + state["sq"])
    send(sq_ref, res_out)
    for c in copies:
        c.wait()


def place_pieces(pieces, t_ref, g_ref, total):
    me = my_index()
    core, q = lax.rem(me, 2), lax.rem(me // 2, 4)
    for m in range(8):
        at = (core ^ (m // 4)) * HALF + (q ^ (m % 4)) * PIECE
        g_ref[pl.ds(pl.multiple_of(at, PIECE), PIECE), :] = pieces[m][...] / total
    n = 0
    for i in range(4):
        rows = slice(128 * i, 128 * i + 64)
        t_ref[rows, 128 * i : 128 * i + 128] = g_ref[64 * n : 64 * n + 64, :]
        n += 1
        for j in range(i + 1, 4):
            t_ref[128 * i : 128 * i + 128, 128 * j : 128 * j + 128] = g_ref[64 * n : 64 * n + 128, :]
            n += 2
    for i in range(4):
        x = g_ref[64 * (n + i // 2) : 64 * (n + i // 2) + 64, :]
        if i % 2 == 0:
            x = pltpu.roll(x, 64, 1)
        t_ref[128 * i + 64 : 128 * i + 128, 128 * i : 128 * i + 128] = x


def fit_call(pieces, data, anchors, total):
    f32 = jnp.float32
    count = len(pieces)
    rows = data.shape[0]

    def body(*refs):
        main_kernel(total, refs[:count], *refs[count:])

    vmem = pl.BlockSpec(memory_space=pltpu.VMEM)
    hbm = pl.BlockSpec(memory_space=pl.ANY)
    return pl.pallas_call(
        body,
        out_shape=(
            jax.ShapeDtypeStruct((512, 512), f32),
            jax.ShapeDtypeStruct((64, 512), f32),
            jax.ShapeDtypeStruct((rows, 512), f32),
            jax.ShapeDtypeStruct((1, 512), f32),
        ),
        in_specs=[vmem] * (count + 2),
        out_specs=(hbm,) * 4,
        scratch_shapes=[
            pltpu.VMEM((512, 512), f32),
            pltpu.VMEM((512, 128), f32),
            pltpu.VMEM((rows, 512), f32),
            pltpu.VMEM((512, 512), f32),
            pltpu.VMEM((64, 128), f32),
            pltpu.VMEM((64, 128), f32),
            pltpu.VMEM((64, 512), f32),
            pltpu.VMEM((64, 512), f32),
            pltpu.VMEM((1, 512), f32),
            pltpu.VMEM((2, 8, 64, 128), f32),
            pltpu.VMEM((2 * HALF, 128), f32),
            pltpu.SemaphoreType.DMA((6 + 4 * -(-rows // 128),)),
        ],
        compiler_params=pltpu.CompilerParams(vmem_limit_bytes=32 << 20),
        name="factor_fit",
    )(*pieces, data, anchors.reshape(64, 1))


def my_index():
    return lax.axis_index("wide") * lax.axis_size("narrow") + lax.axis_index("narrow")


def gram_kernel(x_hbm, own_ref, other_ref, x_ref, both_ref, sem):
    rows = x_ref.shape[0] // 4
    copies = []
    for c in range(4):
        at = pl.ds(rows * c, rows)
        copies.append(pltpu.make_async_copy(x_hbm.at[at, :], x_ref.at[at, :], sem.at[c]))
        copies[-1].start()
    for c in copies:
        c.wait()
    x = x_ref[...]

    def put(n, unit):
        both_ref[n // 9, 64 * (n % 9) : 64 * (n % 9) + 64, :] = unit

    n = 0
    corners = []
    for i in range(4):
        row = mm(x[:, 128 * i : 128 * i + 128], x[:, 128 * i :], TN)
        for j in range(4 - i):
            put(n, row[:64, 128 * j : 128 * j + 128])
            n += 1
            if j:
                put(n, row[64:, 128 * j : 128 * j + 128])
                n += 1
        corners.append(row[64:, :128])
    lanes = lax.broadcasted_iota(jnp.int32, (64, 128), 1)
    for i in (0, 2):
        put(n, jnp.where(lanes < 64, pltpu.roll(corners[i], 64, 1), corners[i + 1]))
        n += 1
    bit = lax.rem(my_index(), 2)
    own_ref[...] = both_ref[bit]
    other_ref[...] = both_ref[1 - bit]


def gram_call(x):
    half = jax.ShapeDtypeStruct((HALF, 128), jnp.float32)
    return pl.pallas_call(
        gram_kernel,
        out_shape=(half, half, jax.ShapeDtypeStruct(x.shape, x.dtype)),
        in_specs=[pl.BlockSpec(memory_space=pltpu.HBM)],
        out_specs=(pl.BlockSpec(memory_space=pltpu.VMEM),) * 3,
        scratch_shapes=[pltpu.VMEM((2, HALF, 128), jnp.float32), pltpu.SemaphoreType.DMA((4,))],
        compiler_params=pltpu.CompilerParams(vmem_limit_bytes=16 << 20),
        name="gram",
    )(pltpu.with_memory_space_constraint(x, pltpu.HBM))


def split_kernel(own_ref, got_ref, *outs):
    q = lax.rem(my_index() // 2, 4)
    for m, out in enumerate(outs):
        rows = pl.ds(pl.multiple_of((q ^ m) * PIECE, PIECE), PIECE)
        out[...] = own_ref[rows, :] + got_ref[rows, :]


def split_call(own, got):
    part = jax.ShapeDtypeStruct((PIECE, 128), jnp.float32)
    return pl.pallas_call(
        split_kernel,
        out_shape=(part,) * 4,
        compiler_params=pltpu.CompilerParams(vmem_limit_bytes=8 << 20),
        name="split",
    )(own, got)


def swap(x, bit, devices):
    return lax.ppermute(x, AXES, [(i, i ^ bit) for i in range(devices)])


def total_gram(x, devices):
    own, other, kept = gram_call(x)
    parts = split_call(own, swap(other, 1, devices))
    got = [swap(parts[m], 2 * m, devices) for m in (1, 2, 3)]
    piece = (parts[0] + got[0]) + (got[1] + got[2])
    bit = 8
    while bit < devices:
        if bit * 2 < devices:
            far = [swap(piece, bit * m, devices) for m in (1, 2, 3)]
            piece = (piece + far[0]) + (far[1] + far[2])
        else:
            piece = piece + swap(piece, bit, devices)
        bit *= 4
    mine = [piece] + [swap(piece, 2 * m, devices) for m in (1, 2, 3)]
    theirs = [swap(p, 1, devices) for p in mine]
    return mine + theirs, kept


def on_device(data, anchors):
    devices = lax.axis_size("wide") * lax.axis_size("narrow")
    pieces, kept = total_gram(data, devices)
    factor, coeffs, basis, resid = fit_call(pieces, kept, anchors, data.shape[0] * devices)
    return (factor, coeffs, basis, resid.reshape(-1))


def solution(mesh):
    placed = (P(AXES, None), P())
    return jax.shard_map(
        on_device,
        mesh=mesh,
        in_specs=placed,
        out_specs=(P(), P(), P(AXES, None), P()),
        check_vma=False,
    )
```

```python
import functools

import jax
import jax.numpy as jnp
from jax import lax
from jax.experimental import pallas as pl
from jax.experimental.pallas import tpu as pltpu
from jax.sharding import PartitionSpec as P

AXES = ("wide", "narrow")
NN = (((1,), (0,)), ((), ()))
NT = (((1,), (1,)), ((), ()))
TN = (((0,), (0,)), ((), ()))
PANEL = 32
HALF = 576
PIECE = HALF // 4
LEFT = (0, 0, 1, 0, 2, 1)
RIGHT = (0, 1, 0, 2, 0, 1)


def thirds(x):
    hi = x.astype(jnp.bfloat16)
    rest = x - hi.astype(jnp.float32)
    mid = rest.astype(jnp.bfloat16)
    low = (rest - mid.astype(jnp.float32)).astype(jnp.bfloat16)
    return (hi, mid, low)


def bdot(a, b, dims):
    return lax.dot_general(a, b, dims, preferred_element_type=jnp.float32)


def six(a, b, dims):
    ca, cb = dims[0][0][0], dims[0][1][0]
    left = jnp.concatenate([a[i] for i in LEFT], axis=ca)
    right = jnp.concatenate([b[i] for i in RIGHT], axis=cb)
    return bdot(left, right, dims)


def mm(a, b, dims=NN):
    return six(thirds(a), thirds(b), dims)


def mm_pick(a, pick, dims):
    return sum(bdot(t, pick, dims) for t in thirds(a))


def rsq(p):
    r = lax.rsqrt(p)
    return r


def lane(x, c):
    return jnp.broadcast_to(x[:, c : c + 1], (8, 128))


def sub(x, i):
    return jnp.take_along_axis(x, jnp.full((8, 128), i, jnp.int32), axis=0, mode="promise_in_bounds")


def eliminate(rows, c0, s_ref):
    a = rows[0][0]
    for k in range(8):
        s_ref[8 * k : 8 * k + 8, :] = lane(a, c0 + k)
    d = {
        (i, k): jnp.broadcast_to(s_ref[8 * k + i : 8 * k + i + 1, :], (8, 128)) for i in range(8) for k in range(i + 1)
    }
    n = [lax.rsqrt(d[i, i]) for i in range(8)]
    d = {(i, k): (v * n[i]) * n[k] for (i, k), v in d.items()}
    ru = [[sub(x, i) * n[i] for x in rows[0]] for i in range(8)]
    cols = [[lane(t[0], c0 + k) * n[k] for k in range(8)] for t in rows[1:]]
    later = [list(t) for t in rows[1:]]
    row = lax.broadcasted_iota(jnp.int32, (8, 128), 0)
    out = [jnp.zeros((8, 128), jnp.float32) for _ in rows[0]]
    low = {}
    for b in (0, 4):
        below = range(b, 8)
        e = {}
        for i in below:
            e[i, 0] = d[i, b]
        p = [d[b, b]]
        for j in range(1, 4):
            for i in range(b + j, 8):
                v = p[0] * d[i, b + j] - e[i, 0] * e[b + j, 0]
                for m in range(1, j):
                    v = p[m] * v - e[i, m] * e[b + j, m]
                e[i, j] = v
            p.append(e[b + j, j])
        rho = [rsq(x) for x in p]
        root = [x * r for x, r in zip(p, rho)]
        inv = [rho[0]]
        acc = root[0]
        for j in range(1, 4):
            inv.append(rho[j] * acc)
            acc = acc * root[j]
        sig = rho[0]
        for j in range(4):
            if j:
                sig = sig * rho[j]
            for i in range(b + j + 1, 8):
                low[i, b + j] = e[i, j] * sig
        if b == 0:
            for i in range(4, 8):
                for k in range(4, i + 1):
                    x = low[i, 0] * low[k, 0] + low[i, 1] * low[k, 1]
                    y = low[i, 2] * low[k, 2] + low[i, 3] * low[k, 3]
                    d[i, k] = d[i, k] - (x + y)
        for j in range(4):
            r, at = inv[j], b + j
            u = [x * r for x in ru[at]]
            for i in range(at + 1, 8):
                ru[i] = [x - low[i, at] * y for x, y in zip(ru[i], u)]
            out = [jnp.where(row == at, y, x) for x, y in zip(out, u)]
            for t, c in enumerate(cols):
                f = c[at] * r
                for k in range(at + 1, 8):
                    c[k] = c[k] - f * low[k, at]
                later[t] = [x - f * y for x, y in zip(later[t], u)]
    return out, later


def tri_upper(x):
    r = lax.broadcasted_iota(jnp.int32, x.shape, 0)
    c = lax.broadcasted_iota(jnp.int32, x.shape, 1)
    return jnp.where(r <= c, x, 0.0)


def eye(n, m):
    r = lax.broadcasted_iota(jnp.int32, (n, m), 0)
    c = lax.broadcasted_iota(jnp.int32, (n, m), 1)
    return (r == c).astype(jnp.float32)


def cholesky_steps(t_ref, e_ref, s_ref, size, blocks, done):
    later = []
    steps = PANEL // 8

    def apply(inverse, rows, c0, width, both):
        at = slice(c0 + 128, c0 + 128 * width)
        parts = ([t_ref[rows, at]] if width > 1 else []) + ([e_ref[rows, :]] if both else [])
        if not parts:
            return
        x = lax.dot_general(
            inverse,
            jnp.concatenate(parts, axis=1),
            NN,
            precision=lax.Precision.HIGHEST,
            preferred_element_type=jnp.float32,
        )
        if width > 1:
            t_ref[rows, at] = x[:, : 128 * (width - 1)]
        if both:
            e_ref[rows, :] = x[:, 128 * (width - 1) :]

    def sides(x):
        split = thirds(x)
        left = jnp.concatenate([split[i] for i in LEFT], axis=0).T
        return left, jnp.concatenate([split[i] for i in RIGHT], axis=0)

    def update(ref, rows, at, left, right):
        ref[rows, at] = ref[rows, at] - bdot(left, right, NN)

    for k in range(blocks):
        r0, c0, width = k * size, k * 128, blocks - k
        e_ref[r0 : r0 + size, :] = eye(size, 128)
        here = slice(c0, c0 + 128)
        for p in range(size // PANEL):
            base = r0 + p * PANEL
            rows = slice(base, base + PANEL)
            tiles = []
            unit = eye(PANEL, 128)
            for t in range(steps):
                tiles.append([t_ref[base + 8 * t : base + 8 * t + 8, here], unit[8 * t : 8 * t + 8, :]])
            outs = []
            for t in range(steps):
                out, tiles = eliminate(tiles, p * PANEL + 8 * t, s_ref.at[(p * steps + t) % 8])
                outs.append(out)
                for _ in range(-(-len(later) // (steps - t))):
                    later.pop(0)()
                yield
            up = jnp.concatenate([o[0] for o in outs], axis=0)
            inverse = jnp.concatenate([o[1] for o in outs], axis=0)[:, :PANEL]
            t_ref[rows, here] = up
            nxt = (p + 1) * PANEL
            last = nxt == size
            if not last:
                left, right = sides(up)
                update(t_ref, slice(base + PANEL, base + 2 * PANEL), here, left[nxt : nxt + PANEL], right)
                if nxt + PANEL < size:
                    later.append(
                        functools.partial(
                            update, t_ref, slice(base + 2 * PANEL, r0 + size), here, left[nxt + PANEL : size], right
                        )
                    )

            def others(left=None, rows=rows, r0=r0, c0=c0, width=width, nxt=nxt, inverse=inverse):
                cols = slice(c0 + 128, c0 + 128 * width)
                w_left, w_right = [], []
                for w in range(1, width):
                    a, b = sides(t_ref[rows, c0 + 128 * w : c0 + 128 * w + 128])
                    w_left.append(a)
                    w_right.append(b)
                if left is not None:
                    e_left, e_right = sides(e_ref[rows, :])
                    in_block = slice(r0 + nxt, r0 + size)
                    if width > 1:
                        update(t_ref, in_block, cols, left[nxt:size], jnp.concatenate(w_right, axis=1))
                    update(e_ref, in_block, slice(0, 128), left[nxt:size], e_right)
                return w_left, w_right

            def below(w_left, w_right, r0=r0, c0=c0, width=width, skip=False):
                for w in range(1, width):
                    at = slice(c0 + 128 * w, c0 + 128 * width)
                    lo = 0
                    right = jnp.concatenate(w_right[w - 1 :], axis=1)
                    if w == 1 and skip:
                        first = slice(r0 + size, r0 + size + PANEL)
                        if width > 2:
                            update(t_ref, first, slice(at.start + 128, at.stop), w_left[0][:PANEL], right[:, 128:])
                        lo = PANEL
                    update(t_ref, slice(r0 + size * w + lo, r0 + size * w + size), at, w_left[w - 1][lo:size], right)

            if last:
                apply(inverse, rows, c0, width, True)
                if width > 1:
                    w_left, w_right = others()
                    update(
                        t_ref,
                        slice(r0 + size, r0 + size + PANEL),
                        slice(c0 + 128, c0 + 256),
                        w_left[0][:PANEL],
                        w_right[0],
                    )
                    later.append(functools.partial(below, w_left, w_right, skip=True))
                done(k)
            else:

                def second(
                    left=left, others=others, below=below, inverse=inverse, rows=rows, c0=c0, width=width
                ):
                    apply(inverse, rows, c0, width, True)
                    held.append(others(left))

                def third(below=below):
                    below(*held.pop(0))

                held = []
                later.append(second)
                if width > 1:
                    later.append(third)


def main_kernel(total, pieces, data_ref, anc_ref, fac_out, coef_out, bas_out, res_out, t_ref, e_ref, y_ref, f_ref, td_ref, ed_ref, rk_ref, cf_ref, sq_ref, s_ref, g_ref, sem):
    nb = 4
    n_rows = data_ref.shape[0]
    copies = []
    queue = []
    state = {}

    def send(src, dst):
        c = pltpu.make_async_copy(src, dst, sem.at[len(copies)])
        c.start()
        copies.append(c)

    place_pieces(pieces, t_ref, g_ref, total)
    lanes = lax.broadcasted_iota(jnp.int32, (64, 512), 1)
    pick = (anc_ref[...] == lanes).astype(jnp.bfloat16)

    def side_steps():
        sums = [None] * nb
        for i in range(nb):
            for j in range(i, nb):
                whole = state["gram"][i, j]
                if i == j:
                    r = lax.broadcasted_iota(jnp.int32, (128, 128), 0)
                    c = lax.broadcasted_iota(jnp.int32, (128, 128), 1)
                    whole = jnp.where((r >= 64) & (c < 64), whole.T, whole)
                g = thirds(whole)
                pi, pj = pick[:, 128 * i : 128 * i + 128], pick[:, 128 * j : 128 * j + 128]
                for x in g:
                    v = bdot(pi, x, NN)
                    sums[j] = v if sums[j] is None else sums[j] + v
                    if i < j:
                        v = bdot(pj, x, NT)
                        sums[i] = v if sums[i] is None else sums[i] + v
                if j % 2:
                    yield
        rows_k = jnp.concatenate(sums, axis=1)
        rk_ref[...] = rows_k
        wide = jnp.concatenate([pick, jnp.zeros((64, 512), jnp.bfloat16)], axis=0)
        td_ref[...] = mm_pick(rows_k, wide, NT)
        yield
        yield from cholesky_steps(td_ref, ed_ref, s_ref.at[1], 64, 1, lambda _: None)
        linv = thirds(ed_ref[:, 0:64])
        z = six(linv, thirds(rk_ref[...]), NN)
        yield
        cf_ref[...] = six(linv, thirds(z), TN)
        send(cf_ref, coef_out)
        state["coef"] = True

    state["gram"] = {
        (i, j): t_ref[128 * i : 128 * i + 128, 128 * j : 128 * j + 128] for i in range(nb) for j in range(i, nb)
    }

    def clear(k):
        if k:
            f_ref[128 * k : 128 * k + 128, 0 : 128 * k] = jnp.zeros((128, 128 * k), jnp.float32)

    for k in range(nb):
        queue.append(functools.partial(clear, k))

    def finished(k):
        lo, hi = 128 * k, 128 * k + 128
        last = k == nb - 1
        src = data_ref if k == 0 else y_ref
        linv = thirds(e_ref[lo:hi, :])
        f_ref[lo:hi, lo:hi] = tri_upper(t_ref[lo:hi, lo:hi])
        if not last:
            f_ref[lo:hi, hi:] = t_ref[lo:hi, hi:]
            above = thirds(t_ref[lo:hi, hi:])

        def rows(n):
            at = slice(128 * n, min(128 * n + 128, n_rows))
            b = six(thirds(src[at, lo:hi]), linv, NT)
            y_ref[at, lo:hi] = b
            if not last:
                y_ref[at, hi:] = src[at, hi:] - six(thirds(b), above, NN)

        def ship_factor():
            send(f_ref.at[lo:hi, :], fac_out.at[lo:hi, :])

        def ship_basis(n):
            at = slice(128 * n, min(128 * n + 128, n_rows))
            send(y_ref.at[at, lo:hi], bas_out.at[at, lo:hi])

        queue.append(ship_factor)
        if last:
            queue.append(functools.partial(residual, k))
        for n in range(-(-n_rows // 128)):
            queue.append(functools.partial(rows, n))
            queue.append(functools.partial(ship_basis, n))
        if not last:
            queue.append(functools.partial(residual, k))

    def residual(k):
        lo, hi = 128 * k, 128 * k + 128
        fk = mm_pick(f_ref[lo:hi, lo:], pick[:, lo:], NT)
        diff = f_ref[lo:hi, :] - six(thirds(fk), thirds(cf_ref[...]), NN)
        v = jnp.sum(diff * diff, axis=0, keepdims=True)
        state["sq"] = v if "sq" not in state else state["sq"] + v

    main = cholesky_steps(t_ref, e_ref, s_ref.at[0], 128, nb, finished)
    side = side_steps()
    running = [main, side]
    while running:
        for s in list(running):
            try:
                next(s)
            except StopIteration:
                running.remove(s)
        if queue:
            queue.pop(0)()
    for f in queue:
        f()
    sq_ref[...] = jnp.sqrt(1.0 + state["sq"])
    send(sq_ref, res_out)
    for c in copies:
        c.wait()


def place_pieces(pieces, t_ref, g_ref, total):
    me = my_index()
    core, q = lax.rem(me, 2), lax.rem(me // 2, 4)
    for m in range(8):
        at = (core ^ (m // 4)) * HALF + (q ^ (m % 4)) * PIECE
        g_ref[pl.ds(pl.multiple_of(at, PIECE), PIECE), :] = pieces[m][...] / total
    n = 0
    for i, first, stop in ((0, 0, 4), (1, 1, 2), (0, 0, 0), (1, 2, 4), (2, 2, 4), (3, 3, 4), (2, 2, 2)):
        for j in range(first, stop):
            tall = 64 if i == j else 128
            t_ref[128 * i : 128 * i + tall, 128 * j : 128 * j + 128] = g_ref[64 * n : 64 * n + tall, :]
            n += tall // 64
        if first == stop:
            x = g_ref[64 * n : 64 * n + 64, :]
            t_ref[128 * i + 64 : 128 * i + 128, 128 * i : 128 * i + 128] = pltpu.roll(x, 64, 1)
            t_ref[128 * i + 192 : 128 * i + 256, 128 * i + 128 : 128 * i + 256] = x
            n += 1

def fit_call(pieces, data, anchors, total):
    f32 = jnp.float32
    count = len(pieces)
    rows = data.shape[0]

    def body(*refs):
        main_kernel(total, refs[:count], *refs[count:])

    vmem = pl.BlockSpec(memory_space=pltpu.VMEM)
    hbm = pl.BlockSpec(memory_space=pl.ANY)
    return pl.pallas_call(
        body,
        out_shape=(
            jax.ShapeDtypeStruct((512, 512), f32),
            jax.ShapeDtypeStruct((64, 512), f32),
            jax.ShapeDtypeStruct((rows, 512), f32),
            jax.ShapeDtypeStruct((1, 512), f32),
        ),
        in_specs=[vmem] * (count + 2),
        out_specs=(hbm,) * 4,
        scratch_shapes=[
            pltpu.VMEM((512, 512), f32),
            pltpu.VMEM((512, 128), f32),
            pltpu.VMEM((rows, 512), f32),
            pltpu.VMEM((512, 512), f32),
            pltpu.VMEM((64, 128), f32),
            pltpu.VMEM((64, 128), f32),
            pltpu.VMEM((64, 512), f32),
            pltpu.VMEM((64, 512), f32),
            pltpu.VMEM((1, 512), f32),
            pltpu.VMEM((2, 8, 64, 128), f32),
            pltpu.VMEM((2 * HALF, 128), f32),
            pltpu.SemaphoreType.DMA((6 + 4 * -(-rows // 128),)),
        ],
        compiler_params=pltpu.CompilerParams(vmem_limit_bytes=32 << 20),
        name="factor_fit",
    )(*pieces, data, anchors.reshape(64, 1))


def my_index():
    return lax.axis_index("wide") * lax.axis_size("narrow") + lax.axis_index("narrow")


def gram_half(x, half, out_ref):
    n = 0

    def put(unit):
        nonlocal n
        out_ref[64 * n : 64 * n + 64, :] = unit
        n += 1

    corners = []
    for i, first, stop in ((0, 0, 4), (1, 1, 2)) if half == 0 else ((1, 2, 4), (2, 2, 4), (3, 3, 4)):
        row = mm(x[:, 128 * i : 128 * i + 128], x[:, 128 * first : 128 * stop], TN)
        for j in range(first, stop):
            block = row[:, 128 * (j - first) : 128 * (j - first) + 128]
            put(block[:64])
            if i == j:
                corners.append(block[64:])
            else:
                put(block[64:])
    lanes = lax.broadcasted_iota(jnp.int32, (64, 128), 1)
    put(jnp.where(lanes < 64, pltpu.roll(corners[0], 64, 1), corners[1]))


def first_kernel(x_hbm, out_ref, x_ref, sem):
    rows = x_ref.shape[0] // 4
    copies = []
    for c in range(4):
        at = pl.ds(rows * c, rows)
        copies.append(pltpu.make_async_copy(x_hbm.at[at, :], x_ref.at[at, :], sem.at[c]))
        copies[-1].start()
    for c in copies:
        c.wait()
    bit = lax.rem(my_index(), 2)
    for half in (0, 1):
        pl.when(bit != half)(lambda half=half: gram_half(x_ref[...], half, out_ref))


def second_kernel(x_ref, out_ref):
    bit = lax.rem(my_index(), 2)
    for half in (0, 1):
        pl.when(bit == half)(lambda half=half: gram_half(x_ref[...], half, out_ref))


def gram_calls(x):
    half = jax.ShapeDtypeStruct((HALF, 128), jnp.float32)
    vmem = pl.BlockSpec(memory_space=pltpu.VMEM)
    cost = pl.CostEstimate(flops=6 * 2 * x.shape[0] * 128 * 640, bytes_accessed=2 << 20, transcendentals=0)
    other, kept = pl.pallas_call(
        first_kernel,
        out_shape=(half, jax.ShapeDtypeStruct(x.shape, x.dtype)),
        in_specs=[pl.BlockSpec(memory_space=pltpu.HBM)],
        out_specs=(vmem, vmem),
        scratch_shapes=[pltpu.SemaphoreType.DMA((4,))],
        compiler_params=pltpu.CompilerParams(vmem_limit_bytes=16 << 20),
        cost_estimate=cost,
        name="gram_other",
    )(pltpu.with_memory_space_constraint(x, pltpu.HBM))
    own = pl.pallas_call(
        second_kernel,
        out_shape=half,
        compiler_params=pltpu.CompilerParams(vmem_limit_bytes=16 << 20),
        cost_estimate=cost,
        name="gram_own",
    )(kept)
    return own, other, kept


def split_kernel(own_ref, got_ref, *outs):
    q = lax.rem(my_index() // 2, 4)
    for m, out in enumerate(outs):
        rows = pl.ds(pl.multiple_of((q ^ m) * PIECE, PIECE), PIECE)
        out[...] = own_ref[rows, :] + got_ref[rows, :]


def split_call(own, got):
    part = jax.ShapeDtypeStruct((PIECE, 128), jnp.float32)
    return pl.pallas_call(
        split_kernel,
        out_shape=(part,) * 4,
        compiler_params=pltpu.CompilerParams(vmem_limit_bytes=8 << 20),
        name="split",
    )(own, got)


def swap(x, bit, devices):
    return lax.ppermute(x, AXES, [(i, i ^ bit) for i in range(devices)])


def total_gram(x, devices):
    own, other, kept = gram_calls(x)
    parts = split_call(own, swap(other, 1, devices))
    got = [swap(parts[m], 2 * m, devices) for m in (1, 2, 3)]
    piece = (parts[0] + got[0]) + (got[1] + got[2])
    bit = 8
    while bit < devices:
        if bit * 2 < devices:
            far = [swap(piece, bit * m, devices) for m in (1, 2, 3)]
            piece = (piece + far[0]) + (far[1] + far[2])
        else:
            piece = piece + swap(piece, bit, devices)
        bit *= 4
    mine = [piece] + [swap(piece, 2 * m, devices) for m in (1, 2, 3)]
    theirs = [swap(p, 1, devices) for p in mine]
    return mine + theirs, kept


def on_device(data, anchors):
    devices = lax.axis_size("wide") * lax.axis_size("narrow")
    pieces, kept = total_gram(data, devices)
    factor, coeffs, basis, resid = fit_call(pieces, kept, anchors, data.shape[0] * devices)
    return (factor, coeffs, basis, resid.reshape(-1))


def solution(mesh):
    placed = (P(AXES, None), P())
    return jax.shard_map(
        on_device,
        mesh=mesh,
        in_specs=placed,
        out_specs=(P(), P(), P(AXES, None), P()),
        check_vma=False,
    )
```

```python
import functools

import jax
import jax.numpy as jnp
from jax import lax
from jax.experimental import pallas as pl
from jax.experimental.pallas import tpu as pltpu
from jax.sharding import PartitionSpec as P

AXES = ("wide", "narrow")
NN = (((1,), (0,)), ((), ()))
NT = (((1,), (1,)), ((), ()))
TN = (((0,), (0,)), ((), ()))
PANEL = 32
HALF = 576
PIECE = HALF // 4
LEFT = (0, 0, 1, 0, 2, 1)
RIGHT = (0, 1, 0, 2, 0, 1)


def thirds(x):
    hi = x.astype(jnp.bfloat16)
    rest = x - hi.astype(jnp.float32)
    mid = rest.astype(jnp.bfloat16)
    low = (rest - mid.astype(jnp.float32)).astype(jnp.bfloat16)
    return (hi, mid, low)


def bdot(a, b, dims):
    return lax.dot_general(a, b, dims, preferred_element_type=jnp.float32)


def six(a, b, dims):
    ca, cb = dims[0][0][0], dims[0][1][0]
    left = jnp.concatenate([a[i] for i in LEFT], axis=ca)
    right = jnp.concatenate([b[i] for i in RIGHT], axis=cb)
    return bdot(left, right, dims)


def mm(a, b, dims=NN):
    return six(thirds(a), thirds(b), dims)


def mm_pick(a, pick, dims):
    return sum(bdot(t, pick, dims) for t in thirds(a))


def rsq(p):
    r = lax.rsqrt(p)
    return r


def lane(x, c):
    return jnp.take_along_axis(x, jnp.full((8, 128), c, jnp.int32), axis=1, mode="promise_in_bounds")


def sub(x, i):
    return jnp.take_along_axis(x, jnp.full((8, 128), i, jnp.int32), axis=0, mode="promise_in_bounds")


def eliminate(rows, c0, s_ref):
    a = rows[0][0]
    for k in range(8):
        s_ref[8 * k : 8 * k + 8, :] = lane(a, c0 + k)
    d = {
        (i, k): jnp.broadcast_to(s_ref[8 * k + i : 8 * k + i + 1, :], (8, 128)) for i in range(8) for k in range(i + 1)
    }
    n = [lax.rsqrt(d[i, i]) for i in range(8)]
    d = {(i, k): (v * n[i]) * n[k] for (i, k), v in d.items()}
    ru = [[sub(x, i) * n[i] for x in rows[0]] for i in range(8)]
    cols = [[lane(t[0], c0 + k) * n[k] for k in range(8)] for t in rows[1:]]
    later = [list(t) for t in rows[1:]]
    row = lax.broadcasted_iota(jnp.int32, (8, 128), 0)
    out = [jnp.zeros((8, 128), jnp.float32) for _ in rows[0]]
    low = {}
    for b in (0, 4):
        below = range(b, 8)
        e = {}
        for i in below:
            e[i, 0] = d[i, b]
        p = [d[b, b]]
        for j in range(1, 4):
            for i in range(b + j, 8):
                v = p[0] * d[i, b + j] - e[i, 0] * e[b + j, 0]
                for m in range(1, j):
                    v = p[m] * v - e[i, m] * e[b + j, m]
                e[i, j] = v
            p.append(e[b + j, j])
        rho = [rsq(x) for x in p]
        root = [x * r for x, r in zip(p, rho)]
        inv = [rho[0]]
        acc = root[0]
        for j in range(1, 4):
            inv.append(rho[j] * acc)
            acc = acc * root[j]
        sig = rho[0]
        for j in range(4):
            if j:
                sig = sig * rho[j]
            for i in range(b + j + 1, 8):
                low[i, b + j] = e[i, j] * sig
        if b == 0:
            for i in range(4, 8):
                for k in range(4, i + 1):
                    x = low[i, 0] * low[k, 0] + low[i, 1] * low[k, 1]
                    y = low[i, 2] * low[k, 2] + low[i, 3] * low[k, 3]
                    d[i, k] = d[i, k] - (x + y)
        for j in range(4):
            r, at = inv[j], b + j
            u = [x * r for x in ru[at]]
            for i in range(at + 1, 8):
                ru[i] = [x - low[i, at] * y for x, y in zip(ru[i], u)]
            out = [jnp.where(row == at, y, x) for x, y in zip(out, u)]
            for t, c in enumerate(cols):
                f = c[at] * r
                for k in range(at + 1, 8):
                    c[k] = c[k] - f * low[k, at]
                later[t] = [x - f * y for x, y in zip(later[t], u)]
    return out, later


def tri_upper(x):
    r = lax.broadcasted_iota(jnp.int32, x.shape, 0)
    c = lax.broadcasted_iota(jnp.int32, x.shape, 1)
    return jnp.where(r <= c, x, 0.0)


def eye(n, m):
    r = lax.broadcasted_iota(jnp.int32, (n, m), 0)
    c = lax.broadcasted_iota(jnp.int32, (n, m), 1)
    return (r == c).astype(jnp.float32)


def cholesky_steps(t_ref, e_ref, s_ref, size, blocks, done):
    later = []
    steps = PANEL // 8

    def apply(inverse, rows, c0, width, both):
        at = slice(c0 + 128, c0 + 128 * width)
        parts = ([t_ref[rows, at]] if width > 1 else []) + ([e_ref[rows, :]] if both else [])
        if not parts:
            return
        x = lax.dot_general(
            inverse,
            jnp.concatenate(parts, axis=1),
            NN,
            precision=lax.Precision.HIGHEST,
            preferred_element_type=jnp.float32,
        )
        if width > 1:
            t_ref[rows, at] = x[:, : 128 * (width - 1)]
        if both:
            e_ref[rows, :] = x[:, 128 * (width - 1) :]

    def sides(x):
        split = thirds(x)
        left = jnp.concatenate([split[i] for i in LEFT], axis=0).T
        return left, jnp.concatenate([split[i] for i in RIGHT], axis=0)

    def update(ref, rows, at, left, right):
        ref[rows, at] = ref[rows, at] - bdot(left, right, NN)

    for k in range(blocks):
        r0, c0, width = k * size, k * 128, blocks - k
        e_ref[r0 : r0 + size, :] = eye(size, 128)
        here = slice(c0, c0 + 128)
        for p in range(size // PANEL):
            base = r0 + p * PANEL
            rows = slice(base, base + PANEL)
            tiles = []
            unit = eye(PANEL, 128)
            for t in range(steps):
                tiles.append([t_ref[base + 8 * t : base + 8 * t + 8, here], unit[8 * t : 8 * t + 8, :]])
            outs = []
            for t in range(steps):
                out, tiles = eliminate(tiles, p * PANEL + 8 * t, s_ref.at[(p * steps + t) % 8])
                outs.append(out)
                for _ in range(-(-len(later) // (steps - t))):
                    later.pop(0)()
                yield
            up = jnp.concatenate([o[0] for o in outs], axis=0)
            inverse = jnp.concatenate([o[1] for o in outs], axis=0)[:, :PANEL]
            t_ref[rows, here] = up
            nxt = (p + 1) * PANEL
            last = nxt == size
            if not last:
                left, right = sides(up)
                update(t_ref, slice(base + PANEL, base + 2 * PANEL), here, left[nxt : nxt + PANEL], right)
                if nxt + PANEL < size:
                    later.append(
                        functools.partial(
                            update, t_ref, slice(base + 2 * PANEL, r0 + size), here, left[nxt + PANEL : size], right
                        )
                    )

            def others(left=None, rows=rows, r0=r0, c0=c0, width=width, nxt=nxt, inverse=inverse):
                cols = slice(c0 + 128, c0 + 128 * width)
                w_left, w_right = [], []
                for w in range(1, width):
                    a, b = sides(t_ref[rows, c0 + 128 * w : c0 + 128 * w + 128])
                    w_left.append(a)
                    w_right.append(b)
                if left is not None:
                    e_left, e_right = sides(e_ref[rows, :])
                    in_block = slice(r0 + nxt, r0 + size)
                    if width > 1:
                        update(t_ref, in_block, cols, left[nxt:size], jnp.concatenate(w_right, axis=1))
                    update(e_ref, in_block, slice(0, 128), left[nxt:size], e_right)
                return w_left, w_right

            def below(w_left, w_right, r0=r0, c0=c0, width=width, skip=False):
                for w in range(1, width):
                    at = slice(c0 + 128 * w, c0 + 128 * width)
                    lo = 0
                    right = jnp.concatenate(w_right[w - 1 :], axis=1)
                    if w == 1 and skip:
                        first = slice(r0 + size, r0 + size + PANEL)
                        if width > 2:
                            update(t_ref, first, slice(at.start + 128, at.stop), w_left[0][:PANEL], right[:, 128:])
                        lo = PANEL
                    update(t_ref, slice(r0 + size * w + lo, r0 + size * w + size), at, w_left[w - 1][lo:size], right)

            if last:
                apply(inverse, rows, c0, width, True)
                if width > 1:
                    w_left, w_right = others()
                    update(
                        t_ref,
                        slice(r0 + size, r0 + size + PANEL),
                        slice(c0 + 128, c0 + 256),
                        w_left[0][:PANEL],
                        w_right[0],
                    )
                    later.append(functools.partial(below, w_left, w_right, skip=True))
                done(k)
            else:

                def second(
                    left=left, others=others, below=below, inverse=inverse, rows=rows, c0=c0, width=width
                ):
                    apply(inverse, rows, c0, width, True)
                    held.append(others(left))

                def third(below=below):
                    below(*held.pop(0))

                held = []
                later.append(second)
                if width > 1:
                    later.append(third)


def main_kernel(total, pieces, data_ref, anc_ref, fac_out, coef_out, bas_out, res_out, t_ref, e_ref, y_ref, f_ref, td_ref, ed_ref, rk_ref, cf_ref, sq_ref, s_ref, g_ref, sem):
    nb = 4
    n_rows = data_ref.shape[0]
    copies = []
    queue = []
    state = {}

    def send(src, dst):
        c = pltpu.make_async_copy(src, dst, sem.at[len(copies)])
        c.start()
        copies.append(c)

    place_pieces(pieces, t_ref, g_ref, total)
    lanes = lax.broadcasted_iota(jnp.int32, (64, 512), 1)
    pick = (anc_ref[...] == lanes).astype(jnp.bfloat16)

    def side_steps():
        sums = [None] * nb
        for i in range(nb):
            for j in range(i, nb):
                whole = state["gram"][i, j]
                if i == j:
                    r = lax.broadcasted_iota(jnp.int32, (128, 128), 0)
                    c = lax.broadcasted_iota(jnp.int32, (128, 128), 1)
                    whole = jnp.where((r >= 64) & (c < 64), whole.T, whole)
                g = thirds(whole)
                pi, pj = pick[:, 128 * i : 128 * i + 128], pick[:, 128 * j : 128 * j + 128]
                for x in g:
                    v = bdot(pi, x, NN)
                    sums[j] = v if sums[j] is None else sums[j] + v
                    if i < j:
                        v = bdot(pj, x, NT)
                        sums[i] = v if sums[i] is None else sums[i] + v
                if j % 2:
                    yield
        rows_k = jnp.concatenate(sums, axis=1)
        rk_ref[...] = rows_k
        wide = jnp.concatenate([pick, jnp.zeros((64, 512), jnp.bfloat16)], axis=0)
        td_ref[...] = mm_pick(rows_k, wide, NT)
        yield
        yield from cholesky_steps(td_ref, ed_ref, s_ref.at[1], 64, 1, lambda _: None)
        linv = thirds(ed_ref[:, 0:64])
        z = six(linv, thirds(rk_ref[...]), NN)
        yield
        cf_ref[...] = six(linv, thirds(z), TN)
        send(cf_ref, coef_out)
        state["coef"] = True

    state["gram"] = {
        (i, j): t_ref[128 * i : 128 * i + 128, 128 * j : 128 * j + 128] for i in range(nb) for j in range(i, nb)
    }

    def clear(k):
        if k:
            f_ref[128 * k : 128 * k + 128, 0 : 128 * k] = jnp.zeros((128, 128 * k), jnp.float32)

    for k in range(nb):
        queue.append(functools.partial(clear, k))

    def finished(k):
        lo, hi = 128 * k, 128 * k + 128
        last = k == nb - 1
        src = data_ref if k == 0 else y_ref
        linv = thirds(e_ref[lo:hi, :])
        f_ref[lo:hi, lo:hi] = tri_upper(t_ref[lo:hi, lo:hi])
        if not last:
            f_ref[lo:hi, hi:] = t_ref[lo:hi, hi:]
            above = thirds(t_ref[lo:hi, hi:])

        def rows(n):
            at = slice(128 * n, min(128 * n + 128, n_rows))
            b = six(thirds(src[at, lo:hi]), linv, NT)
            y_ref[at, lo:hi] = b
            if not last:
                y_ref[at, hi:] = src[at, hi:] - six(thirds(b), above, NN)

        def ship_factor():
            send(f_ref.at[lo:hi, :], fac_out.at[lo:hi, :])

        def ship_basis(n):
            at = slice(128 * n, min(128 * n + 128, n_rows))
            send(y_ref.at[at, lo:hi], bas_out.at[at, lo:hi])

        queue.append(ship_factor)
        if last:
            queue.append(functools.partial(residual, k))
        for n in range(-(-n_rows // 128)):
            queue.append(functools.partial(rows, n))
            queue.append(functools.partial(ship_basis, n))
        if not last:
            queue.append(functools.partial(residual, k))

    def residual(k):
        lo, hi = 128 * k, 128 * k + 128
        fk = mm_pick(f_ref[lo:hi, lo:], pick[:, lo:], NT)
        diff = f_ref[lo:hi, :] - six(thirds(fk), thirds(cf_ref[...]), NN)
        v = jnp.sum(diff * diff, axis=0, keepdims=True)
        state["sq"] = v if "sq" not in state else state["sq"] + v

    main = cholesky_steps(t_ref, e_ref, s_ref.at[0], 128, nb, finished)
    side = side_steps()
    running = [main, side]
    while running:
        for s in list(running):
            try:
                next(s)
            except StopIteration:
                running.remove(s)
        if queue:
            queue.pop(0)()
    for f in queue:
        f()
    sq_ref[...] = jnp.sqrt(1.0 + state["sq"])
    send(sq_ref, res_out)
    for c in copies:
        c.wait()


def place_pieces(pieces, t_ref, g_ref, total):
    me = my_index()
    core, q = lax.rem(me, 2), lax.rem(me // 2, 4)
    for m in range(8):
        at = (core ^ (m // 4)) * HALF + (q ^ (m % 4)) * PIECE
        g_ref[pl.ds(pl.multiple_of(at, PIECE), PIECE), :] = pieces[m][...] / total
    n = 0
    for i, first, stop in ((0, 0, 4), (1, 1, 2), (0, 0, 0), (1, 2, 4), (2, 2, 4), (3, 3, 4), (2, 2, 2)):
        for j in range(first, stop):
            tall = 64 if i == j else 128
            t_ref[128 * i : 128 * i + tall, 128 * j : 128 * j + 128] = g_ref[64 * n : 64 * n + tall, :]
            n += tall // 64
        if first == stop:
            x = g_ref[64 * n : 64 * n + 64, :]
            t_ref[128 * i + 64 : 128 * i + 128, 128 * i : 128 * i + 128] = pltpu.roll(x, 64, 1)
            t_ref[128 * i + 192 : 128 * i + 256, 128 * i + 128 : 128 * i + 256] = x
            n += 1

def fit_call(pieces, data, anchors, total):
    f32 = jnp.float32
    count = len(pieces)
    rows = data.shape[0]

    def body(*refs):
        main_kernel(total, refs[:count], *refs[count:])

    vmem = pl.BlockSpec(memory_space=pltpu.VMEM)
    hbm = pl.BlockSpec(memory_space=pl.ANY)
    return pl.pallas_call(
        body,
        out_shape=(
            jax.ShapeDtypeStruct((512, 512), f32),
            jax.ShapeDtypeStruct((64, 512), f32),
            jax.ShapeDtypeStruct((rows, 512), f32),
            jax.ShapeDtypeStruct((1, 512), f32),
        ),
        in_specs=[vmem] * (count + 2),
        out_specs=(hbm,) * 4,
        scratch_shapes=[
            pltpu.VMEM((512, 512), f32),
            pltpu.VMEM((512, 128), f32),
            pltpu.VMEM((rows, 512), f32),
            pltpu.VMEM((512, 512), f32),
            pltpu.VMEM((64, 128), f32),
            pltpu.VMEM((64, 128), f32),
            pltpu.VMEM((64, 512), f32),
            pltpu.VMEM((64, 512), f32),
            pltpu.VMEM((1, 512), f32),
            pltpu.VMEM((2, 8, 64, 128), f32),
            pltpu.VMEM((2 * HALF, 128), f32),
            pltpu.SemaphoreType.DMA((6 + 4 * -(-rows // 128),)),
        ],
        compiler_params=pltpu.CompilerParams(vmem_limit_bytes=32 << 20),
        name="factor_fit",
    )(*pieces, data, anchors.reshape(64, 1))


def my_index():
    return lax.axis_index("wide") * lax.axis_size("narrow") + lax.axis_index("narrow")


def gram_half(x, half, out_ref):
    n = 0

    def put(unit):
        nonlocal n
        out_ref[64 * n : 64 * n + 64, :] = unit
        n += 1

    corners = []
    for i, first, stop in ((0, 0, 4), (1, 1, 2)) if half == 0 else ((1, 2, 4), (2, 2, 4), (3, 3, 4)):
        row = mm(x[:, 128 * i : 128 * i + 128], x[:, 128 * first : 128 * stop], TN)
        for j in range(first, stop):
            block = row[:, 128 * (j - first) : 128 * (j - first) + 128]
            put(block[:64])
            if i == j:
                corners.append(block[64:])
            else:
                put(block[64:])
    lanes = lax.broadcasted_iota(jnp.int32, (64, 128), 1)
    put(jnp.where(lanes < 64, pltpu.roll(corners[0], 64, 1), corners[1]))


def first_kernel(x_hbm, out_ref, x_ref, sem):
    rows = x_ref.shape[0] // 4
    copies = []
    for c in range(4):
        at = pl.ds(rows * c, rows)
        copies.append(pltpu.make_async_copy(x_hbm.at[at, :], x_ref.at[at, :], sem.at[c]))
        copies[-1].start()
    for c in copies:
        c.wait()
    bit = lax.rem(my_index(), 2)
    for half in (0, 1):
        pl.when(bit != half)(lambda half=half: gram_half(x_ref[...], half, out_ref))


def second_kernel(x_ref, out_ref):
    bit = lax.rem(my_index(), 2)
    for half in (0, 1):
        pl.when(bit == half)(lambda half=half: gram_half(x_ref[...], half, out_ref))


def gram_calls(x):
    half = jax.ShapeDtypeStruct((HALF, 128), jnp.float32)
    vmem = pl.BlockSpec(memory_space=pltpu.VMEM)
    cost = pl.CostEstimate(flops=6 * 2 * x.shape[0] * 128 * 640, bytes_accessed=2 << 20, transcendentals=0)
    other, kept = pl.pallas_call(
        first_kernel,
        out_shape=(half, jax.ShapeDtypeStruct(x.shape, x.dtype)),
        in_specs=[pl.BlockSpec(memory_space=pltpu.HBM)],
        out_specs=(vmem, vmem),
        scratch_shapes=[pltpu.SemaphoreType.DMA((4,))],
        compiler_params=pltpu.CompilerParams(vmem_limit_bytes=16 << 20),
        cost_estimate=cost,
        name="gram_other",
    )(pltpu.with_memory_space_constraint(x, pltpu.HBM))
    own = pl.pallas_call(
        second_kernel,
        out_shape=half,
        compiler_params=pltpu.CompilerParams(vmem_limit_bytes=16 << 20),
        cost_estimate=cost,
        name="gram_own",
    )(kept)
    return own, other, kept


def split_kernel(own_ref, got_ref, *outs):
    q = lax.rem(my_index() // 2, 4)
    for m, out in enumerate(outs):
        rows = pl.ds(pl.multiple_of((q ^ m) * PIECE, PIECE), PIECE)
        out[...] = own_ref[rows, :] + got_ref[rows, :]


def split_call(own, got):
    part = jax.ShapeDtypeStruct((PIECE, 128), jnp.float32)
    return pl.pallas_call(
        split_kernel,
        out_shape=(part,) * 4,
        compiler_params=pltpu.CompilerParams(vmem_limit_bytes=8 << 20),
        name="split",
    )(own, got)


def swap(x, bit, devices):
    return lax.ppermute(x, AXES, [(i, i ^ bit) for i in range(devices)])


def total_gram(x, devices):
    own, other, kept = gram_calls(x)
    parts = split_call(own, swap(other, 1, devices))
    got = [swap(parts[m], 2 * m, devices) for m in (1, 2, 3)]
    piece = (parts[0] + got[0]) + (got[1] + got[2])
    bit = 8
    while bit < devices:
        if bit * 2 < devices:
            far = [swap(piece, bit * m, devices) for m in (1, 2, 3)]
            piece = (piece + far[0]) + (far[1] + far[2])
        else:
            piece = piece + swap(piece, bit, devices)
        bit *= 4
    mine = [piece] + [swap(piece, 2 * m, devices) for m in (1, 2, 3)]
    theirs = [swap(p, 1, devices) for p in mine]
    return mine + theirs, kept


def on_device(data, anchors):
    devices = lax.axis_size("wide") * lax.axis_size("narrow")
    pieces, kept = total_gram(data, devices)
    factor, coeffs, basis, resid = fit_call(pieces, kept, anchors, data.shape[0] * devices)
    return (factor, coeffs, basis, resid.reshape(-1))


def solution(mesh):
    placed = (P(AXES, None), P())
    return jax.shard_map(
        on_device,
        mesh=mesh,
        in_specs=placed,
        out_specs=(P(), P(), P(AXES, None), P()),
        check_vma=False,
    )
```

```python
import functools

import jax
import jax.numpy as jnp
from jax import lax
from jax.experimental import pallas as pl
from jax.experimental.pallas import tpu as pltpu
from jax.sharding import PartitionSpec as P

AXES = ("wide", "narrow")
NN = (((1,), (0,)), ((), ()))
NT = (((1,), (1,)), ((), ()))
TN = (((0,), (0,)), ((), ()))
PANEL = 32
HALF = 576
PIECE = HALF // 4
LEFT = (0, 0, 1, 0, 2, 1)
RIGHT = (0, 1, 0, 2, 0, 1)


def thirds(x):
    hi = x.astype(jnp.bfloat16)
    rest = x - hi.astype(jnp.float32)
    mid = rest.astype(jnp.bfloat16)
    low = (rest - mid.astype(jnp.float32)).astype(jnp.bfloat16)
    return (hi, mid, low)


def bdot(a, b, dims):
    return lax.dot_general(a, b, dims, preferred_element_type=jnp.float32)


def six(a, b, dims):
    ca, cb = dims[0][0][0], dims[0][1][0]
    left = jnp.concatenate([a[i] for i in LEFT], axis=ca)
    right = jnp.concatenate([b[i] for i in RIGHT], axis=cb)
    return bdot(left, right, dims)


def mm(a, b, dims=NN):
    return six(thirds(a), thirds(b), dims)


def mm_pick(a, pick, dims):
    return sum(bdot(t, pick, dims) for t in thirds(a))


def rsq(p):
    r = lax.rsqrt(p)
    return r


def lane(x, c):
    return jnp.take_along_axis(x, jnp.full((8, 128), c, jnp.int32), axis=1, mode="promise_in_bounds")


def sub(x, i):
    return jnp.take_along_axis(x, jnp.full((8, 128), i, jnp.int32), axis=0, mode="promise_in_bounds")


def eliminate(rows, c0, s_ref):
    a = rows[0][0]
    for k in range(8):
        s_ref[8 * k : 8 * k + 8, :] = lane(a, c0 + k)
    d = {
        (i, k): jnp.broadcast_to(s_ref[8 * k + i : 8 * k + i + 1, :], (8, 128)) for i in range(8) for k in range(i + 1)
    }
    n = [lax.rsqrt(d[i, i]) for i in range(8)]
    d = {(i, k): (v * n[i]) * n[k] for (i, k), v in d.items()}
    ru = [[sub(x, i) * n[i] for x in rows[0]] for i in range(8)]
    cols = [[lane(t[0], c0 + k) * n[k] for k in range(8)] for t in rows[1:]]
    later = [list(t) for t in rows[1:]]
    row = lax.broadcasted_iota(jnp.int32, (8, 128), 0)
    out = [jnp.zeros((8, 128), jnp.float32) for _ in rows[0]]
    low = {}
    for b in (0, 4):
        below = range(b, 8)
        e = {}
        for i in below:
            e[i, 0] = d[i, b]
        p = [d[b, b]]
        for j in range(1, 4):
            for i in range(b + j, 8):
                v = p[0] * d[i, b + j] - e[i, 0] * e[b + j, 0]
                for m in range(1, j):
                    v = p[m] * v - e[i, m] * e[b + j, m]
                e[i, j] = v
            p.append(e[b + j, j])
        rho = [rsq(x) for x in p]
        root = [x * r for x, r in zip(p, rho)]
        inv = [rho[0]]
        acc = root[0]
        for j in range(1, 4):
            inv.append(rho[j] * acc)
            acc = acc * root[j]
        sig = rho[0]
        for j in range(4):
            if j:
                sig = sig * rho[j]
            for i in range(b + j + 1, 8):
                low[i, b + j] = e[i, j] * sig
        if b == 0:
            for i in range(4, 8):
                for k in range(4, i + 1):
                    x = low[i, 0] * low[k, 0] + low[i, 1] * low[k, 1]
                    y = low[i, 2] * low[k, 2] + low[i, 3] * low[k, 3]
                    d[i, k] = d[i, k] - (x + y)
        for j in range(4):
            r, at = inv[j], b + j
            u = [x * r for x in ru[at]]
            for i in range(at + 1, 8):
                ru[i] = [x - low[i, at] * y for x, y in zip(ru[i], u)]
            out = [jnp.where(row == at, y, x) for x, y in zip(out, u)]
            for t, c in enumerate(cols):
                f = c[at] * r
                for k in range(at + 1, 8):
                    c[k] = c[k] - f * low[k, at]
                later[t] = [x - f * y for x, y in zip(later[t], u)]
    return out, later


def tri_upper(x):
    r = lax.broadcasted_iota(jnp.int32, x.shape, 0)
    c = lax.broadcasted_iota(jnp.int32, x.shape, 1)
    return jnp.where(r <= c, x, 0.0)


def eye(n, m):
    r = lax.broadcasted_iota(jnp.int32, (n, m), 0)
    c = lax.broadcasted_iota(jnp.int32, (n, m), 1)
    return (r == c).astype(jnp.float32)


def cholesky_steps(t_ref, e_ref, s_ref, size, blocks, done):
    later = []
    steps = PANEL // 8

    def apply(inverse, rows, c0, width, both):
        at = slice(c0 + 128, c0 + 128 * width)
        parts = ([t_ref[rows, at]] if width > 1 else []) + ([e_ref[rows, :]] if both else [])
        if not parts:
            return
        x = lax.dot_general(
            inverse,
            jnp.concatenate(parts, axis=1),
            NN,
            precision=lax.Precision.HIGHEST,
            preferred_element_type=jnp.float32,
        )
        if width > 1:
            t_ref[rows, at] = x[:, : 128 * (width - 1)]
        if both:
            e_ref[rows, :] = x[:, 128 * (width - 1) :]

    def sides(x):
        split = thirds(x)
        left = jnp.concatenate([split[i] for i in LEFT], axis=0).T
        return left, jnp.concatenate([split[i] for i in RIGHT], axis=0)

    def update(ref, rows, at, left, right):
        ref[rows, at] = ref[rows, at] - bdot(left, right, NN)

    for k in range(blocks):
        r0, c0, width = k * size, k * 128, blocks - k
        e_ref[r0 : r0 + size, :] = eye(size, 128)
        here = slice(c0, c0 + 128)
        for p in range(size // PANEL):
            base = r0 + p * PANEL
            rows = slice(base, base + PANEL)
            tiles = []
            unit = eye(PANEL, 128)
            for t in range(steps):
                tiles.append([t_ref[base + 8 * t : base + 8 * t + 8, here], unit[8 * t : 8 * t + 8, :]])
            outs = []
            for t in range(steps):
                out, tiles = eliminate(tiles, p * PANEL + 8 * t, s_ref.at[(p * steps + t) % 8])
                outs.append(out)
                for _ in range(-(-len(later) // (steps - t))):
                    later.pop(0)()
                yield
            up = jnp.concatenate([o[0] for o in outs], axis=0)
            inverse = jnp.concatenate([o[1] for o in outs], axis=0)[:, :PANEL]
            t_ref[rows, here] = up
            nxt = (p + 1) * PANEL
            last = nxt == size
            if not last:
                left, right = sides(up)
                update(t_ref, slice(base + PANEL, base + 2 * PANEL), here, left[nxt : nxt + PANEL], right)
                if nxt + PANEL < size:
                    later.append(
                        functools.partial(
                            update, t_ref, slice(base + 2 * PANEL, r0 + size), here, left[nxt + PANEL : size], right
                        )
                    )

            def others(left=None, rows=rows, r0=r0, c0=c0, width=width, nxt=nxt, inverse=inverse):
                cols = slice(c0 + 128, c0 + 128 * width)
                w_left, w_right = [], []
                for w in range(1, width):
                    a, b = sides(t_ref[rows, c0 + 128 * w : c0 + 128 * w + 128])
                    w_left.append(a)
                    w_right.append(b)
                if left is not None:
                    e_left, e_right = sides(e_ref[rows, :])
                    in_block = slice(r0 + nxt, r0 + size)
                    if width > 1:
                        update(t_ref, in_block, cols, left[nxt:size], jnp.concatenate(w_right, axis=1))
                    update(e_ref, in_block, slice(0, 128), left[nxt:size], e_right)
                return w_left, w_right

            def below(w_left, w_right, r0=r0, c0=c0, width=width, skip=False):
                for w in range(1, width):
                    at = slice(c0 + 128 * w, c0 + 128 * width)
                    lo = 0
                    right = jnp.concatenate(w_right[w - 1 :], axis=1)
                    if w == 1 and skip:
                        first = slice(r0 + size, r0 + size + PANEL)
                        if width > 2:
                            update(t_ref, first, slice(at.start + 128, at.stop), w_left[0][:PANEL], right[:, 128:])
                        lo = PANEL
                    update(t_ref, slice(r0 + size * w + lo, r0 + size * w + size), at, w_left[w - 1][lo:size], right)

            if last:
                apply(inverse, rows, c0, width, True)
                if width > 1:
                    w_left, w_right = others()
                    update(
                        t_ref,
                        slice(r0 + size, r0 + size + PANEL),
                        slice(c0 + 128, c0 + 256),
                        w_left[0][:PANEL],
                        w_right[0],
                    )
                    later.append(functools.partial(below, w_left, w_right, skip=True))
                done(k)
            else:

                def second(
                    left=left, others=others, below=below, inverse=inverse, rows=rows, c0=c0, width=width
                ):
                    apply(inverse, rows, c0, width, True)
                    held.append(others(left))

                def third(below=below):
                    below(*held.pop(0))

                held = []
                later.append(second)
                if width > 1:
                    later.append(third)


def main_kernel(total, pieces, data_ref, anc_ref, fac_out, coef_out, bas_out, res_out, t_ref, e_ref, y_ref, f_ref, td_ref, ed_ref, rk_ref, cf_ref, sq_ref, s_ref, g_ref, sem):
    nb = 4
    n_rows = data_ref.shape[0]
    copies = []
    queue = []
    state = {}

    def send(src, dst):
        c = pltpu.make_async_copy(src, dst, sem.at[len(copies)])
        c.start()
        copies.append(c)

    place_pieces(pieces, t_ref, g_ref, total)
    lanes = lax.broadcasted_iota(jnp.int32, (64, 512), 1)
    pick = (anc_ref[...] == lanes).astype(jnp.bfloat16)

    def side_steps():
        sums = [None] * nb
        for i in range(nb):
            for j in range(i, nb):
                whole = state["gram"][i, j]
                if i == j:
                    r = lax.broadcasted_iota(jnp.int32, (128, 128), 0)
                    c = lax.broadcasted_iota(jnp.int32, (128, 128), 1)
                    whole = jnp.where((r >= 64) & (c < 64), whole.T, whole)
                g = thirds(whole)
                pi, pj = pick[:, 128 * i : 128 * i + 128], pick[:, 128 * j : 128 * j + 128]
                for x in g:
                    v = bdot(pi, x, NN)
                    sums[j] = v if sums[j] is None else sums[j] + v
                    if i < j:
                        v = bdot(pj, x, NT)
                        sums[i] = v if sums[i] is None else sums[i] + v
                if j % 2:
                    yield
        rows_k = jnp.concatenate(sums, axis=1)
        rk_ref[...] = rows_k
        wide = jnp.concatenate([pick, jnp.zeros((64, 512), jnp.bfloat16)], axis=0)
        td_ref[...] = mm_pick(rows_k, wide, NT)
        yield
        yield from cholesky_steps(td_ref, ed_ref, s_ref.at[1], 64, 1, lambda _: None)
        linv = thirds(ed_ref[:, 0:64])
        z = six(linv, thirds(rk_ref[...]), NN)
        yield
        cf_ref[...] = six(linv, thirds(z), TN)
        send(cf_ref, coef_out)
        state["coef"] = True

    state["gram"] = {
        (i, j): t_ref[128 * i : 128 * i + 128, 128 * j : 128 * j + 128] for i in range(nb) for j in range(i, nb)
    }

    def clear(k):
        if k:
            f_ref[128 * k : 128 * k + 128, 0 : 128 * k] = jnp.zeros((128, 128 * k), jnp.float32)

    for k in range(nb):
        queue.append(functools.partial(clear, k))

    def finished(k):
        lo, hi = 128 * k, 128 * k + 128
        last = k == nb - 1
        src = data_ref if k == 0 else y_ref
        linv = thirds(e_ref[lo:hi, :])
        f_ref[lo:hi, lo:hi] = tri_upper(t_ref[lo:hi, lo:hi])
        if not last:
            f_ref[lo:hi, hi:] = t_ref[lo:hi, hi:]
            above = thirds(t_ref[lo:hi, hi:])

        def rows(n):
            at = slice(128 * n, min(128 * n + 128, n_rows))
            b = six(thirds(src[at, lo:hi]), linv, NT)
            y_ref[at, lo:hi] = b
            if not last:
                y_ref[at, hi:] = src[at, hi:] - six(thirds(b), above, NN)

        def ship_factor():
            send(f_ref.at[lo:hi, :], fac_out.at[lo:hi, :])

        def ship_basis(n):
            at = slice(128 * n, min(128 * n + 128, n_rows))
            send(y_ref.at[at, lo:hi], bas_out.at[at, lo:hi])

        queue.append(ship_factor)
        if last:
            queue.append(functools.partial(residual, k))
        for n in range(-(-n_rows // 128)):
            queue.append(functools.partial(rows, n))
            queue.append(functools.partial(ship_basis, n))
        if not last:
            queue.append(functools.partial(residual, k))

    def residual(k):
        lo, hi = 128 * k, 128 * k + 128
        fk = mm_pick(f_ref[lo:hi, lo:], pick[:, lo:], NT)
        diff = f_ref[lo:hi, :] - six(thirds(fk), thirds(cf_ref[...]), NN)
        v = jnp.sum(diff * diff, axis=0, keepdims=True)
        state["sq"] = v if "sq" not in state else state["sq"] + v

    main = cholesky_steps(t_ref, e_ref, s_ref.at[0], 128, nb, finished)
    side = side_steps()
    running = [main, side]
    while running:
        for s in list(running):
            try:
                next(s)
            except StopIteration:
                running.remove(s)
        if queue:
            queue.pop(0)()
    for f in queue:
        f()
    sq_ref[...] = jnp.sqrt(1.0 + state["sq"])
    send(sq_ref, res_out)
    for c in copies:
        c.wait()


def place_pieces(pieces, t_ref, g_ref, total):
    me = my_index()
    core, q = lax.rem(me, 2), lax.rem(me // 2, 4)
    for m in range(8):
        at = (core ^ (m // 4)) * HALF + (q ^ (m % 4)) * PIECE
        g_ref[pl.ds(pl.multiple_of(at, PIECE), PIECE), :] = pieces[m][...] / total
    n = 0
    for i, first, stop in ((0, 0, 4), (1, 1, 2), (0, 0, 0), (1, 2, 4), (2, 2, 4), (3, 3, 4), (2, 2, 2)):
        for j in range(first, stop):
            tall = 64 if i == j else 128
            t_ref[128 * i : 128 * i + tall, 128 * j : 128 * j + 128] = g_ref[64 * n : 64 * n + tall, :]
            n += tall // 64
        if first == stop:
            x = g_ref[64 * n : 64 * n + 64, :]
            t_ref[128 * i + 64 : 128 * i + 128, 128 * i : 128 * i + 128] = pltpu.roll(x, 64, 1)
            t_ref[128 * i + 192 : 128 * i + 256, 128 * i + 128 : 128 * i + 256] = x
            n += 1

def fit_call(pieces, data, anchors, total):
    f32 = jnp.float32
    count = len(pieces)
    rows = data.shape[0]

    def body(*refs):
        main_kernel(total, refs[:count], *refs[count:])

    vmem = pl.BlockSpec(memory_space=pltpu.VMEM)
    hbm = pl.BlockSpec(memory_space=pl.ANY)
    return pl.pallas_call(
        body,
        out_shape=(
            jax.ShapeDtypeStruct((512, 512), f32),
            jax.ShapeDtypeStruct((64, 512), f32),
            jax.ShapeDtypeStruct((rows, 512), f32),
            jax.ShapeDtypeStruct((1, 512), f32),
        ),
        in_specs=[vmem] * (count + 2),
        out_specs=(hbm,) * 4,
        scratch_shapes=[
            pltpu.VMEM((512, 512), f32),
            pltpu.VMEM((512, 128), f32),
            pltpu.VMEM((rows, 512), f32),
            pltpu.VMEM((512, 512), f32),
            pltpu.VMEM((64, 128), f32),
            pltpu.VMEM((64, 128), f32),
            pltpu.VMEM((64, 512), f32),
            pltpu.VMEM((64, 512), f32),
            pltpu.VMEM((1, 512), f32),
            pltpu.VMEM((2, 8, 64, 128), f32),
            pltpu.VMEM((2 * HALF, 128), f32),
            pltpu.SemaphoreType.DMA((6 + 4 * -(-rows // 128),)),
        ],
        compiler_params=pltpu.CompilerParams(vmem_limit_bytes=32 << 20),
        name="factor_fit",
    )(*pieces, data, anchors.reshape(64, 1))


def my_index():
    return lax.axis_index("wide") * lax.axis_size("narrow") + lax.axis_index("narrow")


def gram_half(x, half, out_ref, add=False):
    n = 0

    def put(unit):
        nonlocal n
        at = slice(64 * n, 64 * n + 64)
        out_ref[at, :] = out_ref[at, :] + unit if add else unit
        n += 1

    corners = []
    for i, first, stop in ((0, 0, 4), (1, 1, 2)) if half == 0 else ((1, 2, 4), (2, 2, 4), (3, 3, 4)):
        row = mm(x[:, 128 * i : 128 * i + 128], x[:, 128 * first : 128 * stop], TN)
        for j in range(first, stop):
            block = row[:, 128 * (j - first) : 128 * (j - first) + 128]
            put(block[:64])
            if i == j:
                corners.append(block[64:])
            else:
                put(block[64:])
    lanes = lax.broadcasted_iota(jnp.int32, (64, 128), 1)
    put(jnp.where(lanes < 64, pltpu.roll(corners[0], 64, 1), corners[1]))


def first_kernel(x_hbm, out_ref, x_ref, sem):
    rows = x_ref.shape[0] // 4
    copies = []
    for c in range(4):
        at = pl.ds(rows * c, rows)
        copies.append(pltpu.make_async_copy(x_hbm.at[at, :], x_ref.at[at, :], sem.at[c]))
        copies[-1].start()
    bit = lax.rem(my_index(), 2)
    for part in (0, 1):
        for c in copies[2 * part : 2 * part + 2]:
            c.wait()
        at = slice(2 * rows * part, 2 * rows * part + 2 * rows)
        for half in (0, 1):
            pl.when(bit != half)(
                lambda half=half, at=at, part=part: gram_half(x_ref[at, :], half, out_ref, add=part > 0)
            )


def second_kernel(x_ref, out_ref):
    bit = lax.rem(my_index(), 2)
    for half in (0, 1):
        pl.when(bit == half)(lambda half=half: gram_half(x_ref[...], half, out_ref))


def gram_calls(x):
    half = jax.ShapeDtypeStruct((HALF, 128), jnp.float32)
    vmem = pl.BlockSpec(memory_space=pltpu.VMEM)
    cost = pl.CostEstimate(flops=6 * 2 * x.shape[0] * 128 * 640, bytes_accessed=2 << 20, transcendentals=0)
    other, kept = pl.pallas_call(
        first_kernel,
        out_shape=(half, jax.ShapeDtypeStruct(x.shape, x.dtype)),
        in_specs=[pl.BlockSpec(memory_space=pltpu.HBM)],
        out_specs=(vmem, vmem),
        scratch_shapes=[pltpu.SemaphoreType.DMA((4,))],
        compiler_params=pltpu.CompilerParams(vmem_limit_bytes=16 << 20),
        cost_estimate=cost,
        name="gram_other",
    )(pltpu.with_memory_space_constraint(x, pltpu.HBM))
    own = pl.pallas_call(
        second_kernel,
        out_shape=half,
        compiler_params=pltpu.CompilerParams(vmem_limit_bytes=16 << 20),
        cost_estimate=cost,
        name="gram_own",
    )(kept)
    return own, other, kept


def split_kernel(own_ref, got_ref, *outs):
    q = lax.rem(my_index() // 2, 4)
    for m, out in enumerate(outs):
        rows = pl.ds(pl.multiple_of((q ^ m) * PIECE, PIECE), PIECE)
        out[...] = own_ref[rows, :] + got_ref[rows, :]


def split_call(own, got):
    part = jax.ShapeDtypeStruct((PIECE, 128), jnp.float32)
    return pl.pallas_call(
        split_kernel,
        out_shape=(part,) * 4,
        compiler_params=pltpu.CompilerParams(vmem_limit_bytes=8 << 20),
        name="split",
    )(own, got)


def swap(x, bit, devices):
    return lax.ppermute(x, AXES, [(i, i ^ bit) for i in range(devices)])


def total_gram(x, devices):
    own, other, kept = gram_calls(x)
    parts = split_call(own, swap(other, 1, devices))
    got = [swap(parts[m], 2 * m, devices) for m in (1, 2, 3)]
    piece = (parts[0] + got[0]) + (got[1] + got[2])
    bit = 8
    while bit < devices:
        if bit * 2 < devices:
            far = [swap(piece, bit * m, devices) for m in (1, 2, 3)]
            piece = (piece + far[0]) + (far[1] + far[2])
        else:
            piece = piece + swap(piece, bit, devices)
        bit *= 4
    mine = [piece] + [swap(piece, 2 * m, devices) for m in (1, 2, 3)]
    theirs = [swap(p, 1, devices) for p in mine]
    return mine + theirs, kept


def on_device(data, anchors):
    devices = lax.axis_size("wide") * lax.axis_size("narrow")
    pieces, kept = total_gram(data, devices)
    factor, coeffs, basis, resid = fit_call(pieces, kept, anchors, data.shape[0] * devices)
    return (factor, coeffs, basis, resid.reshape(-1))


def solution(mesh):
    placed = (P(AXES, None), P())
    return jax.shard_map(
        on_device,
        mesh=mesh,
        in_specs=placed,
        out_specs=(P(), P(), P(AXES, None), P()),
        check_vma=False,
    )
```
